512 devices in a mesh: gx: 8 (over y, core), gy: 16 (over z), gz: 4 (over x).
Axes of the slice: x: 4, y: 4, z: 16, core: 2. Of those that a mesh axis runs over, the one named last changes fastest.
Arguments:
- history: float32 [56, 32, 128, 1024], P(None, 'gz', 'gy', 'gx'), may hold values from -6 to 6
- start: float32 [4, 32, 128, 1024], P(None, 'gz', 'gy', 'gx'), may hold values from -51 to 51
- diagonal: float32 [32, 128, 1024], P('gz', 'gy', 'gx'), may hold values from 0.25 to 2
Outputs:
- new_basis: float32 [20, 32, 128, 1024], P(None, 'gz', 'gy', 'gx')
- r_factor: float32 [20, 20], replicated
The draws below stay inside these ranges and needn't reach their ends.
All inputs are finite; a program needn't handle non-finite values.
Results may differ from the reference program's by a relative error of at most 0.0003.
Values sent between devices are 32-bit elements; how exact they have to be, the bound alone decides.
A program may use at most 64 MiB of HBM per device.

```python
import math
import jax
import jax.numpy as jnp
from jax import lax

NRHS = 4
STEPS = 4
HIST = 56
COLS = 20
NX = 1024
NY = 128
NZ = 32


def shared_fields(key):
    first_key = jax.random.fold_in(key, 11)
    second_key = jax.random.fold_in(key, 12)
    hist_vals = jnp.clip(jax.random.normal(first_key, (HIST, NZ, NY, NX), jnp.float32), -6.0, 6.0)
    noise_vals = jnp.clip(jax.random.normal(second_key, (NRHS, NZ, NY, NX), jnp.float32), -6.0, 6.0)
    rise = 2.0
    ramp = 1.0 + rise * jnp.arange(NY, dtype=jnp.float32) / NY
    start_vals = ramp[None, None, :, None] * (0.8 * hist_vals[HIST - NRHS:] + 0.6 * noise_vals)
    return (hist_vals, start_vals)


def draw_history(key, part):
    return shared_fields(key)[0]


def draw_start(key, part):
    return shared_fields(key)[1]


def steps_of(rng, dims, split, smallest, largest):
    gain, own = 1.0, jax.random.fold_in(rng, 6)
    for position, parts in split:
        draws = jnp.exp(jax.random.uniform(jax.random.fold_in(own, position), (parts,), jnp.float32, smallest / len(split), largest / len(split)))
        gain = gain * jnp.repeat(draws, dims[position] // parts).reshape([-1 if axis == position else 1 for axis in range(len(dims))])
    return gain


def setup_inputs(seed: int = 0) -> dict:
    splits = jax.random.split(jax.random.key(seed), 4)
    return {
        "history": draw_history(jax.random.fold_in(splits[3], 71), 0),
        "start": draw_start(jax.random.fold_in(splits[3], 71), 0),
        "diagonal": jnp.clip(jnp.exp(math.log(2.0) - 2.0794415 * jax.random.uniform(splits[2], (NZ, NY, NX), jnp.float32) ** steps_of(splits[2], (NZ, NY, NX), ((0, 4), (1, 16), (2, 8)), -0.2, 0.2)), 0.25, 2.0),
    }


def apply_scaled(field, diagonal):
    padded = jnp.pad(field, ((0, 0), (1, 1), (1, 1), (1, 1)))
    beside = padded[:, 2:, 1:-1, 1:-1] + padded[:, :-2, 1:-1, 1:-1]
    beside = beside + padded[:, 1:-1, 2:, 1:-1] + padded[:, 1:-1, :-2, 1:-1]
    beside = beside + padded[:, 1:-1, 1:-1, 2:] + padded[:, 1:-1, 1:-1, :-2]
    return ((6.0 + diagonal[None]) * field - beside - 7.0 * field) / 7.0

def reference(history, start, diagonal):
    blocks = [start, apply_scaled(start, diagonal)]
    for level in range(1, STEPS):
        blocks.append(2.0 * apply_scaled(blocks[level], diagonal) - blocks[level - 1])
    basis = jnp.concatenate(blocks, axis=0)
    cell_total = float(NX * NY * NZ)
    flat_basis = basis.reshape(COLS, -1)
    flat_hist = history.reshape(HIST, -1)
    coef = jnp.dot(flat_hist.astype(jnp.float32), flat_basis.T.astype(jnp.float32), precision=lax.Precision.HIGHEST, preferred_element_type=jnp.float32) / cell_total
    projected = flat_basis - jnp.dot(coef.T.astype(jnp.float32), flat_hist.astype(jnp.float32), precision=lax.Precision.HIGHEST, preferred_element_type=jnp.float32)
    gram = jnp.dot(projected.astype(jnp.float32), projected.T.astype(jnp.float32), precision=lax.Precision.HIGHEST, preferred_element_type=jnp.float32) / cell_total
    lower = jnp.linalg.cholesky(gram)
    solved = lax.linalg.triangular_solve(lower, projected, left_side=True, lower=True)
    return (solved.reshape(basis.shape), lower.T)
```

```python
import functools

import jax
import jax.numpy as jnp
from jax import lax
from jax.experimental import pallas as pl
from jax.experimental.pallas import tpu as pltpu
from jax.sharding import PartitionSpec as P

STEPS = 4
NRHS = 4
HIST = 56
COLS = 20
MESH = pl.DeviceIdType.MESH
F32 = jnp.float32
BF16 = jnp.bfloat16
NT = (((1,), (1,)), ((), ()))
NN = (((1,), (0,)), ((), ()))
HIGH = lax.Precision.HIGHEST


def iota(shape, dim):
    return lax.broadcasted_iota(jnp.int32, shape, dim)


def split(value):
    top = value.astype(BF16)
    return top, (value - top.astype(F32)).astype(BF16)


def bdot(left, right, dims):
    return lax.dot_general(left, right, dims, preferred_element_type=F32)


def fdot(left, right, dims):
    return lax.dot_general(left, right, dims, precision=HIGH, preferred_element_type=F32)


def keep_same_row(value):
    same = (iota(value.shape, 0) % 8) == (iota(value.shape, 1) % 8)
    masked = jnp.where(same, value, 0.0)
    return jnp.sum(masked.reshape(value.shape[0] // 8, 8, value.shape[1]), axis=1)


class Exchange:
    def __init__(self, axis, count, send, recv):
        self.axis, self.count, self.send, self.recv = axis, count, send, recv
        self.me = lax.axis_index(axis)

    def peer(self, step):
        return lax.rem(self.me + step, self.count)

    def copy(self, step, src, dst):
        return pltpu.make_async_remote_copy(
            src_ref=src,
            dst_ref=dst,
            send_sem=self.send.at[step - 1],
            recv_sem=self.recv.at[self.me],
            device_id={self.axis: self.peer(step)},
            device_id_type=MESH,
        )

    def start(self, src_of, dst):
        for step in range(1, self.count):
            self.copy(step, src_of(self.peer(step)), dst).start()

    def wait_recv(self, slot_of):
        for step in range(1, self.count):
            source = self.peer(step)
            slot = slot_of(source)
            pltpu.make_async_remote_copy(
                src_ref=slot,
                dst_ref=slot,
                send_sem=self.send.at[step - 1],
                recv_sem=self.recv.at[source],
                device_id={self.axis: source},
                device_id_type=MESH,
            ).wait_recv()

    def wait_send(self, src_of, dst):
        for step in range(1, self.count):
            self.copy(step, src_of(self.peer(step)), dst).wait_send()


def total_of(ref, count):
    total = ref[0]
    for place in range(1, count):
        total = total + ref[place]
    return total


def power_kernel(
    nx, ny, nz,
    hist_hbm, start_hbm, diag_hbm,
    xcat, cout, gout,
    wbuf, hbuf, ebuf, halo_z, halo_y, halo_x, pack_y, pack_x,
    gloc, g_x, gs_x, g_z, gs_z, g_y, gs_y, ga_z,
    cloc, c_x, c_z, c_y, cs_y,
    load_sem, hs_sem, hr_sem,
    gxs, gxr, gzs, gzr, gys, gyr, gas, gar, gbs, gbr,
    cxs, cxr, czs, czr, cys, cyr, cas, car,
):
    ix, iy, iz = lax.axis_index("gx"), lax.axis_index("gy"), lax.axis_index("gz")
    load_w = pltpu.make_async_copy(start_hbm, wbuf.at[pl.ds(0, NRHS)], load_sem.at[0])
    load_d = pltpu.make_async_copy(diag_hbm, ebuf, load_sem.at[1])
    load_h = pltpu.make_async_copy(hist_hbm, hbuf, load_sem.at[2])
    load_w.start()
    load_d.start()
    load_h.start()

    for which in range(2):
        edge_x = ix == (0 if which == 0 else nx - 1)
        edge_y = iy == (0 if which == 0 else ny - 1)
        edge_z = iz == (0 if which == 0 else nz - 1)

        @pl.when(edge_x)
        def _():
            for level in range(STEPS):
                halo_x[level, which] = jnp.zeros((8, 128), F32)

        @pl.when(edge_y)
        def _():
            for level in range(STEPS):
                halo_y[level, which] = jnp.zeros((32, 128), F32)

        @pl.when(edge_z)
        def _():
            for level in range(STEPS):
                halo_z[level, which] = jnp.zeros((NRHS, 8, 128), F32)

    barrier = pltpu.get_barrier_semaphore()
    for axis, me, count in (("gz", iz, nz), ("gx", ix, nx), ("gy", iy, ny)):
        for step in range(1, count):
            pl.semaphore_signal(
                barrier, inc=1, device_id={axis: lax.rem(me + step, count)}, device_id_type=MESH
            )

    lane = iota((8, 128), 1)
    row = iota((8, 128), 0)

    def faces(level):
        packed = jnp.zeros((8, 128), F32)
        low_rows, high_rows = [], []
        for f in range(NRHS):
            for z in range(8):
                v = wbuf[NRHS * level + f, z]
                n = 2 * (8 * f + z)
                turned = v if n == 0 else pltpu.roll(v, n, 1)
                packed = jnp.where((lane == n) | (lane == (n + 127) % 128), turned, packed)
                low_rows.append(v[0:1])
                high_rows.append(v[7:8])
        pack_x[level] = packed
        pack_y[level, 0] = jnp.concatenate(low_rows, axis=0)
        pack_y[level, 1] = jnp.concatenate(high_rows, axis=0)

    def halo_copies(level):
        block = pl.ds(NRHS * level, NRHS)
        out = []
        for which, step in ((1, -1), (0, 1)):
            has_x = (ix > 0) if step < 0 else (ix < nx - 1)
            has_y = (iy > 0) if step < 0 else (iy < ny - 1)
            has_z = (iz > 0) if step < 0 else (iz < nz - 1)
            for number, has, axis, me, count, src, dst in (
                (0, has_z, "gz", iz, nz, wbuf.at[block, 0 if step < 0 else 7], halo_z),
                (1, has_y, "gy", iy, ny, pack_y.at[level, 1 - which], halo_y),
                (2, has_x, "gx", ix, nx, pack_x.at[level], halo_x),
            ):
                out.append((
                    has,
                    which,
                    number,
                    pltpu.make_async_remote_copy(
                        src_ref=src,
                        dst_ref=dst.at[level, which],
                        send_sem=hs_sem.at[level, which, number],
                        recv_sem=hr_sem.at[level, which, number],
                        device_id={axis: lax.rem(me + step + count, count)},
                        device_id_type=MESH,
                    ),
                ))
        return out

    def send_halos(level):
        for has, _, _, copy in halo_copies(level):
            @pl.when(has)
            def _():
                copy.start()

    def wait_halos(level):
        for _, which, number, copy in halo_copies(level):
            me, count = ((iz, nz), (iy, ny), (ix, nx))[number]
            has = (me > 0) if which == 0 else (me < count - 1)

            @pl.when(has)
            def _():
                copy.wait_recv()

    def finish_halos(level):
        for has, _, _, copy in halo_copies(level):
            @pl.when(has)
            def _():
                copy.wait_send()

    def keep_split(level):
        for z in range(8):
            block = wbuf[NRHS * level:NRHS * (level + 1), z].reshape(8 * NRHS, 128)
            top, low = split(block)
            rows = pl.ds(8 * (HIST + NRHS * level), 8 * NRHS)
            xcat[rows, 128 * z:128 * (z + 1)] = top
            xcat[rows, 1024 + 128 * z:1024 + 128 * (z + 1)] = low

    def advance(level):
        left, right = halo_x[level, 0], halo_x[level, 1]
        both = jnp.where(lane % 2 == 1, left, right)
        for f in range(NRHS):
            for z in range(8):
                n = 2 * (8 * f + z)
                at = NRHS * level + f
                v = wbuf[at, z]
                turned = both if n == 0 else pltpu.roll(both, 128 - n, 1)
                beside = pltpu.roll(jnp.where(lane == 127, turned, v), 1, 1)
                beside = beside + pltpu.roll(jnp.where(lane == 0, turned, v), 127, 1)
                low = halo_y[level, 0, 8 * f + z:8 * f + z + 1]
                high = halo_y[level, 1, 8 * f + z:8 * f + z + 1]
                beside = beside + jnp.where(row == 0, low, pltpu.roll(v, 1, 0))
                beside = beside + jnp.where(row == 7, high, pltpu.roll(v, 7, 0))
                beside = beside + (halo_z[level, 0, f] if z == 0 else wbuf[at, z - 1])
                beside = beside + (halo_z[level, 1, f] if z == 7 else wbuf[at, z + 1])
                scaled = ebuf[z] * v - beside * (1.0 / 7.0)
                if level > 0:
                    scaled = 2.0 * scaled - wbuf[at - NRHS, z]
                wbuf[at + NRHS, z] = scaled

    load_w.wait()
    faces(0)
    load_d.wait()
    ebuf[...] = (ebuf[...] - 1.0) * (1.0 / 7.0)
    load_h.wait()
    for z in range(8):
        top, low = split(hbuf[:, z].reshape(8 * HIST, 128))
        xcat[0:8 * HIST, 128 * z:128 * (z + 1)] = top
        xcat[0:8 * HIST, 1024 + 128 * z:1024 + 128 * (z + 1)] = low
    keep_split(0)

    pl.semaphore_wait(barrier, (nx - 1) + (ny - 1) + (nz - 1))
    send_halos(0)

    top, low = xcat[0:8 * HIST, 0:1024], xcat[0:8 * HIST, 1024:2048]
    pairs = bdot(top, top, NT) + bdot(top, low, NT) + bdot(low, top, NT)
    rows = keep_same_row(pairs)
    pick = (iota((8 * HIST, 128), 0) // 8) == iota((8 * HIST, 128), 1)
    pick2 = (iota((8 * HIST, 128), 0) // 8) == (iota((8 * HIST, 128), 1) - 64)
    folded = fdot(rows[0:32], pick.astype(F32), NN)
    tail = fdot(rows[32:56], pick2.astype(F32), NN)
    folded = folded + jnp.concatenate([tail, jnp.zeros((8, 128), F32)], axis=0)
    for r in range(32):
        gloc[r] = folded[r:r + 1]

    a, b, c = g_x.shape[1], g_z.shape[1], c_x.shape[1]
    e_gx = Exchange("gx", nx, gxs, gxr)
    e_gz = Exchange("gz", nz, gzs, gzr)
    e_gy = Exchange("gy", ny, gys, gyr)
    e_ga = Exchange("gz", nz, gas, gar)
    e_gb = Exchange("gx", nx, gbs, gbr)
    e_cx = Exchange("gx", nx, cxs, cxr)
    e_cz = Exchange("gz", nz, czs, czr)
    e_cy = Exchange("gy", ny, cys, cyr)
    e_ca = Exchange("gx", nx, cas, car)

    gx_src = lambda peer: gloc.at[pl.ds(a * peer, a)]
    gz_src = lambda peer: gs_x.at[pl.ds(b * peer, b)]
    cx_src = lambda peer: cloc.at[pl.ds(c * peer, c)]

    g_x[ix] = gloc[pl.ds(a * ix, a)]
    e_gx.start(gx_src, g_x.at[ix])

    wait_halos(0)
    advance(0)
    faces(1)
    send_halos(1)
    keep_split(1)
    e_gx.wait_recv(lambda s: g_x.at[s])
    gs_x[...] = total_of(g_x, nx)
    g_z[iz] = gs_x[pl.ds(b * iz, b)]
    e_gz.start(gz_src, g_z.at[iz])

    wait_halos(1)
    advance(1)
    faces(2)
    send_halos(2)
    keep_split(2)
    e_gz.wait_recv(lambda s: g_z.at[s])
    gs_z[...] = total_of(g_z, nz)
    g_y[iy] = gs_z[...]
    e_gy.start(lambda peer: gs_z, g_y.at[iy])

    wait_halos(2)
    advance(2)
    faces(3)
    send_halos(3)
    keep_split(3)

    wait_halos(3)
    advance(3)
    keep_split(4)

    wt = xcat[8 * HIST:8 * (HIST + COLS), 0:1024]
    wl = xcat[8 * HIST:8 * (HIST + COLS), 1024:2048]
    xt, xl = xcat[:, 0:1024], xcat[:, 1024:2048]
    pairs = bdot(xt, wt, NT) + bdot(xt, wl, NT) + bdot(xl, wt, NT)
    rows = keep_same_row(pairs)
    rows = jnp.concatenate([rows, jnp.zeros((128 - HIST - COLS, 8 * COLS), F32)], axis=0)
    pick = iota((24, 8 * COLS), 0) == (iota((24, 8 * COLS), 1) // 8)
    products = fdot(pick.astype(F32), rows, NT)
    for r in range(24):
        cloc[r] = products[r:r + 1]
    c_x[ix] = cloc[pl.ds(c * ix, c)]
    e_cx.start(cx_src, c_x.at[ix])

    e_gy.wait_recv(lambda s: g_y.at[s])
    gs_y[...] = total_of(g_y, ny)
    ga_z[pl.ds(b * iz, b)] = gs_y[...]
    e_ga.start(lambda peer: gs_y, ga_z.at[pl.ds(b * iz, b)])

    e_cx.wait_recv(lambda s: c_x.at[s])
    c_z[iz] = total_of(c_x, nx)
    e_cz.start(lambda peer: c_z.at[iz], c_z.at[iz])

    e_ga.wait_recv(lambda s: ga_z.at[pl.ds(b * s, b)])
    gout[pl.ds(a * ix, a)] = ga_z[...]
    e_gb.start(lambda peer: ga_z, gout.at[pl.ds(a * ix, a)])

    e_cz.wait_recv(lambda s: c_z.at[s])
    c_y[iy] = total_of(c_z, nz)
    e_cy.start(lambda peer: c_y.at[iy], c_y.at[iy])

    e_gb.wait_recv(lambda s: gout.at[pl.ds(a * s, a)])
    for level in range(STEPS):
        finish_halos(level)

    e_cy.wait_recv(lambda s: c_y.at[s])
    cs_y[...] = total_of(c_y, ny)
    cout[pl.ds(c * ix, c)] = cs_y[...]
    e_ca.start(lambda peer: cs_y, cout.at[pl.ds(c * ix, c)])

    e_gx.wait_send(gx_src, g_x.at[ix])
    e_gz.wait_send(gz_src, g_z.at[iz])
    e_gy.wait_send(lambda peer: gs_z, g_y.at[iy])
    e_ga.wait_send(lambda peer: gs_y, ga_z.at[pl.ds(b * iz, b)])
    e_gb.wait_send(lambda peer: ga_z, gout.at[pl.ds(a * ix, a)])
    e_cx.wait_send(cx_src, c_x.at[ix])
    e_cz.wait_send(lambda peer: c_z.at[iz], c_z.at[iz])
    e_cy.wait_send(lambda peer: c_y.at[iy], c_y.at[iy])
    e_ca.wait_recv(lambda s: cout.at[pl.ds(c * s, c)])
    e_ca.wait_send(lambda peer: cs_y, cout.at[pl.ds(c * ix, c)])


def finish_kernel(cells, xcat, cout, gout, new_basis, r_factor):
    lane = iota((24, 128), 1)
    row = iota((24, 128), 0)
    scale = 1.0 / cells
    coef = cout[...].reshape(24, 128) * scale
    folded = gout[...].reshape(32, 128) * scale
    turned = pltpu.roll(folded, 64, 1)
    hist_gram = jnp.concatenate([folded, turned[0:24]], axis=0)
    hist_gram = jnp.where(iota((HIST, 128), 1) < HIST, hist_gram, 0.0)
    coef_h = jnp.where(lane < HIST, coef, 0.0)
    work = fdot(coef_h[:, 0:HIST], hist_gram, NN)
    wide = jnp.concatenate([coef_h, jnp.zeros((104, 128), F32)], axis=0)
    gram = fdot(work - 2.0 * coef_h, wide, NT)
    gram = gram + jnp.where(lane < COLS, pltpu.roll(coef, 128 - HIST, 1), 0.0)
    rhs = jnp.where(lane < HIST, -coef, jnp.where(lane - HIST == row, 1.0, 0.0))

    columns = [jnp.broadcast_to(gram[:, k:k + 1], (24, 128)) for k in range(COLS)]
    lower = jnp.zeros((24, 128), F32)
    for j in range(COLS):
        pivot = jnp.broadcast_to(columns[j][j:j + 1], (24, 128))
        inverse = lax.rsqrt(pivot)
        inverse = inverse * (1.5 - 0.5 * pivot * inverse * inverse)
        column = jnp.where(row >= j, columns[j] * inverse, 0.0)
        lower = jnp.where(lane == j, column, lower)
        solved = jnp.broadcast_to(rhs[j:j + 1], (24, 128)) * inverse
        rhs = jnp.where(row == j, solved, rhs - jnp.where(row > j, column * solved, 0.0))
        for k in range(j + 1, COLS):
            columns[k] = columns[k] - column * jnp.broadcast_to(column[k:k + 1], (24, 128))
    square = jnp.concatenate([lower, jnp.zeros((104, 128), F32)], axis=0)
    r_factor[...] = square.T[0:COLS, 0:COLS]

    weights = rhs[0:COLS]
    top, low = split(weights)
    spread = ((iota((128, 8 * (HIST + COLS)), 1) // 8) == iota((128, 8 * (HIST + COLS)), 0)).astype(BF16)
    size = (8 * COLS, 8 * (HIST + COLS))
    same = (iota(size, 0) % 8) == (iota(size, 1) % 8)

    def widen(part):
        wide = bdot(part, spread, NN)
        wide = jnp.broadcast_to(wide[:, None, :], (COLS, 8, size[1])).reshape(size)
        return jnp.where(same, wide, 0.0).astype(BF16)

    top, low = widen(top), widen(low)
    for part in range(4):
        cols = slice(256 * part, 256 * (part + 1))
        lows = slice(1024 + 256 * part, 1024 + 256 * (part + 1))
        out = bdot(top, xcat[:, cols], NN) + bdot(top, xcat[:, lows], NN) + bdot(low, xcat[:, cols], NN)
        for half in range(2):
            new_basis[:, 2 * part + half] = out[:, 128 * half:128 * (half + 1)].reshape(COLS, 8, 128)


def on_device(nx, ny, nz, history, start, diagonal):
    a = 32 // nx
    b = a // nz
    c = 24 // nx
    dma = pltpu.SemaphoreType.DMA
    row = lambda *shape: pltpu.VMEM((*shape, 1, 128), F32)
    any_spec = pl.BlockSpec(memory_space=pl.ANY)
    vmem = pl.BlockSpec(memory_space=pltpu.VMEM)
    xcat, cout, gout = pl.pallas_call(
        functools.partial(power_kernel, nx, ny, nz),
        name="powers",
        out_shape=(
            jax.ShapeDtypeStruct((8 * (HIST + COLS), 2048), BF16),
            jax.ShapeDtypeStruct((24, 1, 128), F32),
            jax.ShapeDtypeStruct((32, 1, 128), F32),
        ),
        in_specs=[any_spec] * 3,
        out_specs=(vmem, vmem, vmem),
        scratch_shapes=[
            pltpu.VMEM((COLS, 8, 8, 128), F32),
            pltpu.VMEM((HIST, 8, 8, 128), F32),
            pltpu.VMEM((8, 8, 128), F32),
            pltpu.VMEM((STEPS, 2, NRHS, 8, 128), F32),
            pltpu.VMEM((STEPS, 2, 32, 128), F32),
            pltpu.VMEM((STEPS, 2, 8, 128), F32),
            pltpu.VMEM((STEPS, 2, 32, 128), F32),
            pltpu.VMEM((STEPS, 8, 128), F32),
            row(32), row(nx, a), row(a), row(nz, b), row(b), row(ny, b), row(b), row(a),
            row(24), row(nx, c), row(nz, c), row(ny, c), row(c),
            dma((3,)), dma((STEPS, 2, 3)), dma((STEPS, 2, 3)),
            dma((nx,)), dma((nx,)), dma((nz,)), dma((nz,)), dma((ny,)), dma((ny,)),
            dma((nz,)), dma((nz,)), dma((nx,)), dma((nx,)),
            dma((nx,)), dma((nx,)), dma((nz,)), dma((nz,)), dma((ny,)), dma((ny,)),
            dma((nx,)), dma((nx,)),
        ],
        compiler_params=pltpu.CompilerParams(
            collective_id=0, has_side_effects=True, vmem_limit_bytes=24 * 1024 * 1024
        ),
    )(history, start, diagonal)
    cells = float(nx * ny * nz * diagonal.size)
    return pl.pallas_call(
        functools.partial(finish_kernel, cells),
        name="finish",
        out_shape=(
            jax.ShapeDtypeStruct((COLS, 8, 8, 128), F32),
            jax.ShapeDtypeStruct((COLS, COLS), F32),
        ),
        in_specs=[vmem] * 3,
        out_specs=(vmem, vmem),
        compiler_params=pltpu.CompilerParams(vmem_limit_bytes=24 * 1024 * 1024),
    )(xcat, cout, gout)


def solution(mesh):
    return jax.shard_map(
        functools.partial(on_device, mesh.shape["gx"], mesh.shape["gy"], mesh.shape["gz"]),
        mesh=mesh,
        in_specs=(P(None, "gz", "gy", "gx"), P(None, "gz", "gy", "gx"), P("gz", "gy", "gx")),
        out_specs=(P(None, "gz", "gy", "gx"), P()),
        check_vma=False,
    )
```

```python
import functools

import jax
import jax.numpy as jnp
from jax import lax
from jax.experimental import pallas as pl
from jax.experimental.pallas import tpu as pltpu
from jax.sharding import PartitionSpec as P

STEPS = 4
NRHS = 4
HIST = 56
COLS = 20
MESH = pl.DeviceIdType.MESH
F32 = jnp.float32
BF16 = jnp.bfloat16
NT = (((1,), (1,)), ((), ()))
NN = (((1,), (0,)), ((), ()))
HIGH = lax.Precision.HIGHEST
VMEM_BYTES = 66_300_000


def iota(shape, dim):
    return lax.broadcasted_iota(jnp.int32, shape, dim)


def split(value):
    top = value.astype(BF16)
    return top, (value - top.astype(F32)).astype(BF16)


def bdot(left, right, dims):
    return lax.dot_general(left, right, dims, preferred_element_type=F32)


def fdot(left, right, dims):
    return lax.dot_general(left, right, dims, precision=HIGH, preferred_element_type=F32)


def keep_same_row(value):
    same = (iota(value.shape, 0) % 8) == (iota(value.shape, 1) % 8)
    masked = jnp.where(same, value, 0.0)
    return jnp.sum(masked.reshape(value.shape[0] // 8, 8, value.shape[1]), axis=1)


def thirds(value):
    first = value.astype(BF16)
    rest = value - first.astype(F32)
    second = rest.astype(BF16)
    return first, second, (rest - second.astype(F32)).astype(BF16)


class Total:
    def __init__(self, sizes, loc, inp, plane, line, out, send, recv):
        self.nx, self.ny, self.nz = sizes
        self.loc, self.inp, self.plane, self.line, self.out = loc, inp, plane, line, out
        self.send, self.recv = send, recv
        self.ix, self.iy, self.iz = lax.axis_index("gx"), lax.axis_index("gy"), lax.axis_index("gz")
        self.core = lax.rem(self.ix, 2)
        self.iyc = self.ix // 2

    def pair_copy(self, src, dst, number):
        return pltpu.make_async_remote_copy(
            src_ref=src, dst_ref=dst, send_sem=self.send.at[number], recv_sem=self.recv.at[number],
            device_id={"gx": self.ix + 1 - 2 * self.core}, device_id_type=MESH,
        )

    def plane_copies(self):
        nyc, nz = self.nx // 2, self.nz
        for step in range(1, nyc * nz):
            py = lax.rem(self.iyc + step // nz, nyc)
            pz = lax.rem(self.iz + step % nz, nz)
            yield py * nz + pz, self.iyc * nz + self.iz, {"gx": 2 * py + self.core, "gz": pz}, 2 + step

    def line_copies(self):
        for step in range(1, self.ny):
            peer = lax.rem(self.iy + step, self.ny)
            yield peer, self.iy, {"gy": peer}, 2 + (self.nx // 2) * self.nz + step

    def spread(self, copies, buf, base):
        for peer, me, device, number in copies:
            pltpu.make_async_remote_copy(
                src_ref=buf.at[me], dst_ref=buf.at[me], send_sem=self.send.at[number],
                recv_sem=self.recv.at[base + me], device_id=device, device_id_type=MESH,
            ).start()

    def collect(self, copies, buf, base):
        for peer, _, device, number in copies:
            pltpu.make_async_remote_copy(
                src_ref=buf.at[peer], dst_ref=buf.at[peer], send_sem=self.send.at[number],
                recv_sem=self.recv.at[base + peer], device_id=device, device_id_type=MESH,
            ).wait_recv()

    def drain(self, copies, buf, base):
        for peer, me, device, number in copies:
            pltpu.make_async_remote_copy(
                src_ref=buf.at[me], dst_ref=buf.at[me], send_sem=self.send.at[number],
                recv_sem=self.recv.at[base + me], device_id=device, device_id_type=MESH,
            ).wait_send()

    def first(self):
        return self.pair_copy(self.loc.at[1 - self.core], self.inp, 0)

    def last(self):
        return self.pair_copy(self.out.at[self.core], self.out.at[self.core], 1)

    def start_pair(self):
        self.first().start()

    def start_plane(self):
        self.first().wait_recv()
        self.plane[self.iyc * self.nz + self.iz] = self.loc[self.core] + self.inp[...]
        self.spread(self.plane_copies(), self.plane, 2)

    def start_line(self):
        self.collect(self.plane_copies(), self.plane, 2)
        self.line[self.iy] = total_of(self.plane)
        self.spread(self.line_copies(), self.line, 2 + (self.nx // 2) * self.nz)

    def start_share(self):
        self.collect(self.line_copies(), self.line, 2 + (self.nx // 2) * self.nz)
        self.out[self.core] = total_of(self.line)
        self.last().start()

    def result(self):
        other = self.out.at[1 - self.core]
        self.pair_copy(other, other, 1).wait_recv()
        return self.out[0], self.out[1]

    def finish(self):
        self.first().wait_send()
        self.drain(self.plane_copies(), self.plane, 2)
        self.drain(self.line_copies(), self.line, 2 + (self.nx // 2) * self.nz)
        self.last().wait_send()


def total_of(ref):
    parts = [ref[place] for place in range(ref.shape[0])]
    while len(parts) > 1:
        parts = [sum(parts[k:k + 2][1:], parts[k]) for k in range(0, len(parts), 2)]
    return parts[0]


def fold_history(pairs):
    rows = jnp.concatenate(thirds(keep_same_row(pairs)), axis=0)
    pick = ((iota((8 * HIST, 128), 0) // 8) == iota((8 * HIST, 128), 1)).astype(BF16)
    parts = bdot(rows, pick, NN)
    full = parts[0:HIST] + parts[HIST:2 * HIST] + parts[2 * HIST:3 * HIST]
    lane = iota((8, 128), 1)
    tiles = []
    for half in range(2):
        low = 8 * half
        tile = jnp.where(lane < 56, full[low:low + 8], 0.0)
        tile = jnp.where((lane >= 56) & (lane < 96), pltpu.roll(full[16 + low:24 + low], 40, 1), tile)
        tile = jnp.where((lane >= 96) & (lane < 120), pltpu.roll(full[32 + low:40 + low], 64, 1), tile)
        if half == 0:
            tile = jnp.where(lane >= 120, pltpu.roll(full[48:56], 72, 1), tile)
        tiles.append(tile)
    return tiles


def unfold_history(tiles):
    lane = iota((8, 128), 1)
    rows = []
    for first, turn in ((0, 0), (16, 88), (32, 64), (48, 56)):
        for tile in tiles[:1] if first == 48 else tiles:
            turned = tile if turn == 0 else pltpu.roll(tile, turn, 1)
            rows.append(jnp.where((lane >= first) & (lane < HIST), turned, 0.0))
    upper = jnp.concatenate(rows, axis=0)
    right = jnp.where(iota((HIST, 128), 1) >= 16 * (iota((HIST, 128), 0) // 16) + 16, upper, 0.0)
    return upper, right


def fold_basis(pairs):
    rows = keep_same_row(pairs)
    rows = jnp.concatenate([rows, jnp.zeros((128 - HIST - COLS, 8 * COLS), F32)], axis=0)
    rows = jnp.concatenate(thirds(rows), axis=0)
    pick = (iota((24, 8 * COLS), 0) == (iota((24, 8 * COLS), 1) // 8)).astype(BF16)
    parts = bdot(pick, rows, NT)
    full = parts[:, 0:128] + parts[:, 128:256] + parts[:, 256:384]
    lane = iota((8, 128), 1)
    one = jnp.where(lane < HIST, full[0:8], jnp.where(lane >= 64, pltpu.roll(full[8:16], 64, 1), 0.0))
    two = jnp.where(lane < HIST, full[16:24], 0.0)
    for part in range(3):
        first = 64 + 20 * part
        turned = pltpu.roll(full[8 * part:8 * part + 8], first - HIST, 1)
        two = jnp.where((lane >= first) & (lane < first + COLS), turned, two)
    return one, two


def unfold_basis(one, two):
    lane = iota((24, 128), 1)
    coef = jnp.concatenate([one, pltpu.roll(one, 64, 1), two], axis=0)
    own = jnp.concatenate([pltpu.roll(two, 128 - 64 - 20 * part, 1) for part in range(3)], axis=0)
    return jnp.where(lane < HIST, coef, 0.0), jnp.where(lane < COLS, own, 0.0)


def cycle_kernel(
    nx, ny, nz,
    hist_hbm, start_hbm, diag_hbm,
    kept, sums,
    xcat, wbuf, hbuf, ebuf, halo_z, halo_y, halo_x, pack_y, pack_x,
    g_loc, g_inp, g_plane, g_line, g_out,
    c_loc, c_inp, c_plane, c_line, c_out,
    load_sem, hs_sem, hr_sem, g_send, g_recv, c_send, c_recv,
):
    sizes = (nx, ny, nz)
    gsum = Total(sizes, g_loc, g_inp, g_plane, g_line, g_out, g_send, g_recv)
    csum = Total(sizes, c_loc, c_inp, c_plane, c_line, c_out, c_send, c_recv)
    ix, iy, iz = lax.axis_index("gx"), lax.axis_index("gy"), lax.axis_index("gz")
    load_w = pltpu.make_async_copy(start_hbm, wbuf.at[pl.ds(0, NRHS)], load_sem.at[0])
    load_d = pltpu.make_async_copy(diag_hbm, ebuf, load_sem.at[1])
    load_h = pltpu.make_async_copy(hist_hbm, hbuf, load_sem.at[2])
    load_w.start()
    load_d.start()
    load_h.start()

    for which in range(2):
        edge_x = ix == (0 if which == 0 else nx - 1)
        edge_y = iy == (0 if which == 0 else ny - 1)
        edge_z = iz == (0 if which == 0 else nz - 1)

        @pl.when(edge_x)
        def _():
            for level in range(STEPS):
                halo_x[level, which] = jnp.zeros((8, 128), F32)

        @pl.when(edge_y)
        def _():
            for level in range(STEPS):
                halo_y[level, which] = jnp.zeros((32, 128), F32)

        @pl.when(edge_z)
        def _():
            for level in range(STEPS):
                halo_z[level, which] = jnp.zeros((NRHS, 8, 128), F32)

    barrier = pltpu.get_barrier_semaphore()
    greeted = [device for _, _, device, _ in gsum.plane_copies()]
    greeted += [device for _, _, device, _ in gsum.line_copies()]
    greeted += [{"gx": lax.rem(ix + 1, nx)}, {"gx": lax.rem(ix + nx - 1, nx)}]
    for device in greeted:
        pl.semaphore_signal(barrier, inc=1, device_id=device, device_id_type=MESH)

    lane = iota((8, 128), 1)
    row = iota((8, 128), 0)

    def faces(level):
        packed = jnp.zeros((8, 128), F32)
        low_rows, high_rows = [], []
        for f in range(NRHS):
            for z in range(8):
                v = wbuf[NRHS * level + f, z]
                n = 2 * (8 * f + z)
                turned = v if n == 0 else pltpu.roll(v, n, 1)
                packed = jnp.where((lane == n) | (lane == (n + 127) % 128), turned, packed)
                low_rows.append(v[0:1])
                high_rows.append(v[7:8])
        pack_x[level] = packed
        pack_y[level, 0] = jnp.concatenate(low_rows, axis=0)
        pack_y[level, 1] = jnp.concatenate(high_rows, axis=0)

    def halo_copies(level):
        block = pl.ds(NRHS * level, NRHS)
        out = []
        for which, step in ((1, -1), (0, 1)):
            has_x = (ix > 0) if step < 0 else (ix < nx - 1)
            has_y = (iy > 0) if step < 0 else (iy < ny - 1)
            has_z = (iz > 0) if step < 0 else (iz < nz - 1)
            for number, has, axis, me, count, src, dst in (
                (0, has_z, "gz", iz, nz, wbuf.at[block, 0 if step < 0 else 7], halo_z),
                (1, has_y, "gy", iy, ny, pack_y.at[level, 1 - which], halo_y),
                (2, has_x, "gx", ix, nx, pack_x.at[level], halo_x),
            ):
                out.append((
                    has,
                    which,
                    number,
                    pltpu.make_async_remote_copy(
                        src_ref=src,
                        dst_ref=dst.at[level, which],
                        send_sem=hs_sem.at[level, which, number],
                        recv_sem=hr_sem.at[level, which, number],
                        device_id={axis: lax.rem(me + step + count, count)},
                        device_id_type=MESH,
                    ),
                ))
        return out

    def send_halos(level):
        for has, _, _, copy in halo_copies(level):
            @pl.when(has)
            def _():
                copy.start()

    def wait_halos(level):
        for _, which, number, copy in halo_copies(level):
            me, count = ((iz, nz), (iy, ny), (ix, nx))[number]
            has = (me > 0) if which == 0 else (me < count - 1)

            @pl.when(has)
            def _():
                copy.wait_recv()

    def finish_halos(level):
        for has, _, _, copy in halo_copies(level):
            @pl.when(has)
            def _():
                copy.wait_send()

    def keep_split(level):
        for z in range(8):
            block = wbuf[NRHS * level:NRHS * (level + 1), z].reshape(8 * NRHS, 128)
            top, low = split(block)
            rows = pl.ds(8 * (HIST + NRHS * level), 8 * NRHS)
            xcat[rows, 128 * z:128 * (z + 1)] = top
            xcat[rows, 1024 + 128 * z:1024 + 128 * (z + 1)] = low

    def advance(level):
        left, right = halo_x[level, 0], halo_x[level, 1]
        both = jnp.where(lane % 2 == 1, left, right)
        for f in range(NRHS):
            for z in range(8):
                n = 2 * (8 * f + z)
                at = NRHS * level + f
                v = wbuf[at, z]
                turned = both if n == 0 else pltpu.roll(both, 128 - n, 1)
                beside = pltpu.roll(jnp.where(lane == 127, turned, v), 1, 1)
                beside = beside + pltpu.roll(jnp.where(lane == 0, turned, v), 127, 1)
                low = halo_y[level, 0, 8 * f + z:8 * f + z + 1]
                high = halo_y[level, 1, 8 * f + z:8 * f + z + 1]
                beside = beside + jnp.where(row == 0, low, pltpu.roll(v, 1, 0))
                beside = beside + jnp.where(row == 7, high, pltpu.roll(v, 7, 0))
                beside = beside + (halo_z[level, 0, f] if z == 0 else wbuf[at, z - 1])
                beside = beside + (halo_z[level, 1, f] if z == 7 else wbuf[at, z + 1])
                scaled = ebuf[z] * v - beside * (1.0 / 7.0)
                if level > 0:
                    scaled = 2.0 * scaled - wbuf[at - NRHS, z]
                wbuf[at + NRHS, z] = scaled

    load_w.wait()
    faces(0)
    pl.semaphore_wait(barrier, len(greeted))
    send_halos(0)
    load_d.wait()
    ebuf[...] = (ebuf[...] - 1.0) * (1.0 / 7.0)
    load_h.wait()
    for z in range(8):
        top, low = split(hbuf[:, z].reshape(8 * HIST, 128))
        xcat[0:8 * HIST, 128 * z:128 * (z + 1)] = top
        xcat[0:8 * HIST, 1024 + 128 * z:1024 + 128 * (z + 1)] = low

    wait_halos(0)
    advance(0)
    faces(1)
    send_halos(1)
    top, low = xcat[0:8 * HIST, 0:1024], xcat[0:8 * HIST, 1024:2048]
    pairs = bdot(top, top, NT) + bdot(top, low, NT) + bdot(low, top, NT)
    g_loc[0], g_loc[1] = fold_history(pairs)
    gsum.start_pair()

    wait_halos(1)
    advance(1)
    faces(2)
    send_halos(2)
    gsum.start_plane()
    keep_split(0)
    keep_split(1)

    wait_halos(2)
    advance(2)
    faces(3)
    send_halos(3)
    gsum.start_line()
    keep_split(2)
    keep_split(3)

    wait_halos(3)
    advance(3)
    keep_split(4)
    store = pltpu.make_async_copy(xcat, kept, load_sem.at[0])
    store.start()

    wt = xcat[8 * HIST:8 * (HIST + COLS), 0:1024]
    wl = xcat[8 * HIST:8 * (HIST + COLS), 1024:2048]
    xt, xl = xcat[:, 0:1024], xcat[:, 1024:2048]
    pairs = bdot(xt, wt, NT) + bdot(xt, wl, NT) + bdot(xl, wt, NT)
    c_loc[0], c_loc[1] = fold_basis(pairs)
    csum.start_pair()
    csum.start_plane()
    gsum.start_share()
    csum.start_line()
    for level in range(STEPS):
        finish_halos(level)
    sums[2], sums[3] = gsum.result()
    gsum.finish()
    csum.start_share()
    store.wait()
    sums[0], sums[1] = csum.result()
    csum.finish()


def finish_kernel(cells, kept, sums, new_basis, r_factor, xcat, done, load_sem, store_sem):
    load = pltpu.make_async_copy(kept, xcat, load_sem.at[0])
    load.start()
    scale = 1.0 / cells
    one, two, three, four = [sums[k] * scale for k in range(4)]
    gram_h, right_h = unfold_history([three, four])
    lane = iota((24, 128), 1)
    row = iota((24, 128), 0)
    coef, own = unfold_basis(one, two)
    work = fdot(coef[:, 0:HIST], gram_h, NN) + fdot(coef, jnp.concatenate([right_h, jnp.zeros((72, 128), F32)], axis=0), NT)
    wide = jnp.concatenate([coef, jnp.zeros((104, 128), F32)], axis=0)
    gram = fdot(work - 2.0 * coef, wide, NT) + own
    rhs = jnp.where(lane < HIST, -coef, jnp.where(lane - HIST == row, 1.0, 0.0))

    columns = [jnp.broadcast_to(gram[:, k:k + 1], (24, 128)) for k in range(COLS)]
    lower = jnp.zeros((24, 128), F32)
    for j in range(COLS):
        pivot = jnp.broadcast_to(columns[j][j:j + 1], (24, 128))
        inverse = lax.rsqrt(pivot)
        inverse = inverse * (1.5 - 0.5 * pivot * inverse * inverse)
        column = jnp.where(row >= j, columns[j] * inverse, 0.0)
        lower = jnp.where(lane == j, column, lower)
        solved = jnp.broadcast_to(rhs[j:j + 1], (24, 128)) * inverse
        rhs = jnp.where(row == j, solved, rhs - jnp.where(row > j, column * solved, 0.0))
        for k in range(j + 1, COLS):
            columns[k] = columns[k] - column * jnp.broadcast_to(column[k:k + 1], (24, 128))
    square = jnp.concatenate([lower, jnp.zeros((104, 128), F32)], axis=0)
    r_factor[...] = square.T[0:COLS, 0:COLS]

    weights = rhs[0:COLS]
    top, low = split(weights)
    spread = ((iota((128, 8 * (HIST + COLS)), 1) // 8) == iota((128, 8 * (HIST + COLS)), 0)).astype(BF16)
    size = (8 * COLS, 8 * (HIST + COLS))
    same = (iota(size, 0) % 8) == (iota(size, 1) % 8)

    def widen(part):
        wide = bdot(part, spread, NN)
        wide = jnp.broadcast_to(wide[:, None, :], (COLS, 8, size[1])).reshape(size)
        return jnp.where(same, wide, 0.0).astype(BF16)

    top, low = widen(top), widen(low)
    load.wait()
    stores = []
    for part in range(4):
        cols = slice(256 * part, 256 * (part + 1))
        lows = slice(1024 + 256 * part, 1024 + 256 * (part + 1))
        out = bdot(top, xcat[:, cols], NN) + bdot(top, xcat[:, lows], NN) + bdot(low, xcat[:, cols], NN)
        for half in range(2):
            done[:, 2 * part + half] = out[:, 128 * half:128 * (half + 1)].reshape(COLS, 8, 128)
        layers = pl.ds(2 * part, 2)
        stores.append(pltpu.make_async_copy(done.at[:, layers], new_basis.at[:, layers], store_sem.at[part]))
        stores[-1].start()
    for copy in stores:
        copy.wait()


def on_device(nx, ny, nz, history, start, diagonal):
    dma = pltpu.SemaphoreType.DMA
    tiles = lambda *shape: pltpu.VMEM((*shape, 8, 128), F32)
    plane = (nx // 2) * nz
    reduction = [tiles(2), tiles(), tiles(plane), tiles(ny), tiles(2)]
    any_spec = pl.BlockSpec(memory_space=pl.ANY)
    vmem = pl.BlockSpec(memory_space=pltpu.VMEM)
    cells = float(nx * ny * nz * diagonal.size)
    kept, sums = pl.pallas_call(
        functools.partial(cycle_kernel, nx, ny, nz),
        name="cycle",
        out_shape=(
            jax.ShapeDtypeStruct((8 * (HIST + COLS), 2048), BF16),
            jax.ShapeDtypeStruct((4, 8, 128), F32),
        ),
        in_specs=[any_spec] * 3,
        out_specs=(any_spec, vmem),
        scratch_shapes=[
            pltpu.VMEM((8 * (HIST + COLS), 2048), BF16),
            tiles(COLS, 8),
            tiles(HIST, 8),
            tiles(8),
            tiles(STEPS, 2, NRHS),
            pltpu.VMEM((STEPS, 2, 32, 128), F32),
            tiles(STEPS, 2),
            pltpu.VMEM((STEPS, 2, 32, 128), F32),
            tiles(STEPS),
            *reduction,
            *reduction,
            dma((3,)), dma((STEPS, 2, 3)), dma((STEPS, 2, 3)),
            *[dma((2 + plane + ny,))] * 4,
        ],
        compiler_params=pltpu.CompilerParams(
            collective_id=0, has_side_effects=True, vmem_limit_bytes=VMEM_BYTES
        ),
    )(history, start, diagonal)
    return pl.pallas_call(
        functools.partial(finish_kernel, cells),
        name="finish",
        out_shape=(
            jax.ShapeDtypeStruct((COLS, 8, 8, 128), F32),
            jax.ShapeDtypeStruct((COLS, COLS), F32),
        ),
        in_specs=[any_spec, vmem],
        out_specs=(any_spec, vmem),
        scratch_shapes=[pltpu.VMEM((8 * (HIST + COLS), 2048), BF16), tiles(COLS, 8), dma((1,)), dma((4,))],
        compiler_params=pltpu.CompilerParams(vmem_limit_bytes=VMEM_BYTES),
    )(kept, sums)


def solution(mesh):
    return jax.shard_map(
        functools.partial(on_device, mesh.shape["gx"], mesh.shape["gy"], mesh.shape["gz"]),
        mesh=mesh,
        in_specs=(P(None, "gz", "gy", "gx"), P(None, "gz", "gy", "gx"), P("gz", "gy", "gx")),
        out_specs=(P(None, "gz", "gy", "gx"), P()),
        check_vma=False,
    )
```

```python
import functools

import jax
import jax.numpy as jnp
from jax import lax
from jax.experimental import pallas as pl
from jax.experimental.pallas import tpu as pltpu
from jax.sharding import PartitionSpec as P

STEPS = 4
NRHS = 4
HIST = 56
COLS = 20
MESH = pl.DeviceIdType.MESH
F32 = jnp.float32
BF16 = jnp.bfloat16
NT = (((1,), (1,)), ((), ()))
NN = (((1,), (0,)), ((), ()))
HIGH = lax.Precision.HIGHEST
VMEM_BYTES = 66_300_000


def iota(shape, dim):
    return lax.broadcasted_iota(jnp.int32, shape, dim)


def split(value):
    top = value.astype(BF16)
    return top, (value - top.astype(F32)).astype(BF16)


def bdot(left, right, dims):
    return lax.dot_general(left, right, dims, preferred_element_type=F32)


def fdot(left, right, dims):
    return lax.dot_general(left, right, dims, precision=HIGH, preferred_element_type=F32)


def keep_same_row(value):
    same = (iota(value.shape, 0) % 8) == (iota(value.shape, 1) % 8)
    masked = jnp.where(same, value, 0.0)
    return jnp.sum(masked.reshape(value.shape[0] // 8, 8, value.shape[1]), axis=1)


def thirds(value):
    first = value.astype(BF16)
    rest = value - first.astype(F32)
    second = rest.astype(BF16)
    return first, second, (rest - second.astype(F32)).astype(BF16)


class Total:
    def __init__(self, sizes, loc, inp, plane, line, out, send, recv):
        self.nx, self.ny, self.nz = sizes
        self.loc, self.inp, self.plane, self.line, self.out = loc, inp, plane, line, out
        self.send, self.recv = send, recv
        self.ix, self.iy, self.iz = lax.axis_index("gx"), lax.axis_index("gy"), lax.axis_index("gz")
        self.core = lax.rem(self.ix, 2)
        self.iyc = self.ix // 2

    def pair_copy(self, src, dst, number):
        return pltpu.make_async_remote_copy(
            src_ref=src, dst_ref=dst, send_sem=self.send.at[number], recv_sem=self.recv.at[number],
            device_id={"gx": self.ix + 1 - 2 * self.core}, device_id_type=MESH,
        )

    def plane_copies(self):
        nyc, nz = self.nx // 2, self.nz
        for step in range(1, nyc * nz):
            py = lax.rem(self.iyc + step // nz, nyc)
            pz = lax.rem(self.iz + step % nz, nz)
            yield py * nz + pz, self.iyc * nz + self.iz, {"gx": 2 * py + self.core, "gz": pz}, 2 + step

    def line_copies(self):
        for step in range(1, self.ny):
            peer = lax.rem(self.iy + step, self.ny)
            yield peer, self.iy, {"gy": peer}, 2 + (self.nx // 2) * self.nz + step

    def spread(self, copies, buf, base):
        for peer, me, device, number in copies:
            pltpu.make_async_remote_copy(
                src_ref=buf.at[me], dst_ref=buf.at[me], send_sem=self.send.at[number],
                recv_sem=self.recv.at[base + me], device_id=device, device_id_type=MESH,
            ).start()

    def collect(self, copies, buf, base):
        for peer, _, device, number in copies:
            pltpu.make_async_remote_copy(
                src_ref=buf.at[peer], dst_ref=buf.at[peer], send_sem=self.send.at[number],
                recv_sem=self.recv.at[base + peer], device_id=device, device_id_type=MESH,
            ).wait_recv()

    def drain(self, copies, buf, base):
        for peer, me, device, number in copies:
            pltpu.make_async_remote_copy(
                src_ref=buf.at[me], dst_ref=buf.at[me], send_sem=self.send.at[number],
                recv_sem=self.recv.at[base + me], device_id=device, device_id_type=MESH,
            ).wait_send()

    def first(self):
        return self.pair_copy(self.loc.at[1 - self.core], self.inp, 0)

    def last(self):
        return self.pair_copy(self.out.at[self.core], self.out.at[self.core], 1)

    def start_pair(self):
        self.first().start()

    def start_plane(self):
        self.first().wait_recv()
        self.plane[self.iyc * self.nz + self.iz] = self.loc[self.core] + self.inp[...]
        self.spread(self.plane_copies(), self.plane, 2)

    def start_line(self):
        self.collect(self.plane_copies(), self.plane, 2)
        self.line[self.iy] = total_of(self.plane)
        self.spread(self.line_copies(), self.line, 2 + (self.nx // 2) * self.nz)

    def start_share(self):
        self.collect(self.line_copies(), self.line, 2 + (self.nx // 2) * self.nz)
        self.out[self.core] = total_of(self.line)
        self.last().start()

    def result(self):
        other = self.out.at[1 - self.core]
        self.pair_copy(other, other, 1).wait_recv()
        return self.out[0], self.out[1]

    def finish(self):
        self.first().wait_send()
        self.drain(self.plane_copies(), self.plane, 2)
        self.drain(self.line_copies(), self.line, 2 + (self.nx // 2) * self.nz)
        self.last().wait_send()


def total_of(ref):
    parts = [ref[place] for place in range(ref.shape[0])]
    while len(parts) > 1:
        parts = [sum(parts[k:k + 2][1:], parts[k]) for k in range(0, len(parts), 2)]
    return parts[0]


def fold_history(pairs):
    rows = jnp.concatenate(thirds(keep_same_row(pairs)), axis=0)
    pick = ((iota((8 * HIST, 128), 0) // 8) == iota((8 * HIST, 128), 1)).astype(BF16)
    parts = bdot(rows, pick, NN)
    full = parts[0:HIST] + parts[HIST:2 * HIST] + parts[2 * HIST:3 * HIST]
    lane = iota((8, 128), 1)
    tiles = []
    for half in range(2):
        low = 8 * half
        tile = jnp.where(lane < 56, full[low:low + 8], 0.0)
        tile = jnp.where((lane >= 56) & (lane < 96), pltpu.roll(full[16 + low:24 + low], 40, 1), tile)
        tile = jnp.where((lane >= 96) & (lane < 120), pltpu.roll(full[32 + low:40 + low], 64, 1), tile)
        if half == 0:
            tile = jnp.where(lane >= 120, pltpu.roll(full[48:56], 72, 1), tile)
        tiles.append(tile)
    return tiles


def unfold_history(tiles):
    lane = iota((8, 128), 1)
    rows = []
    for first, turn in ((0, 0), (16, 88), (32, 64), (48, 56)):
        for tile in tiles[:1] if first == 48 else tiles:
            turned = tile if turn == 0 else pltpu.roll(tile, turn, 1)
            rows.append(jnp.where((lane >= first) & (lane < HIST), turned, 0.0))
    upper = jnp.concatenate(rows, axis=0)
    right = jnp.where(iota((HIST, 128), 1) >= 16 * (iota((HIST, 128), 0) // 16) + 16, upper, 0.0)
    return upper, right


def fold_basis(pairs):
    rows = keep_same_row(pairs)
    rows = jnp.concatenate([rows, jnp.zeros((128 - HIST - COLS, 8 * COLS), F32)], axis=0)
    rows = jnp.concatenate(thirds(rows), axis=0)
    pick = (iota((24, 8 * COLS), 0) == (iota((24, 8 * COLS), 1) // 8)).astype(BF16)
    parts = bdot(pick, rows, NT)
    full = parts[:, 0:128] + parts[:, 128:256] + parts[:, 256:384]
    lane = iota((8, 128), 1)
    one = jnp.where(lane < HIST, full[0:8], jnp.where(lane >= 64, pltpu.roll(full[8:16], 64, 1), 0.0))
    two = jnp.where(lane < HIST, full[16:24], 0.0)
    for part in range(3):
        first = 64 + 20 * part
        turned = pltpu.roll(full[8 * part:8 * part + 8], first - HIST, 1)
        two = jnp.where((lane >= first) & (lane < first + COLS), turned, two)
    return one, two


def unfold_basis(one, two):
    lane = iota((24, 128), 1)
    coef = jnp.concatenate([one, pltpu.roll(one, 64, 1), two], axis=0)
    own = jnp.concatenate([pltpu.roll(two, 128 - 64 - 20 * part, 1) for part in range(3)], axis=0)
    return jnp.where(lane < HIST, coef, 0.0), jnp.where(lane < COLS, own, 0.0)


def cycle_kernel(
    nx, ny, nz,
    hist_hbm, start_hbm, diag_hbm,
    kept, sums,
    xcat, hbuf, main, side, edge, corner, x_send, x_recv, x_own, e_recv, k_recv, weight_main, weight_side,
    g_loc, g_inp, g_plane, g_line, g_out,
    c_loc, c_inp, c_plane, c_line, c_out,
    load_sem, hs_sem, hr_sem, g_send, g_recv, c_send, c_recv,
):
    sizes = (nx, ny, nz)
    gsum = Total(sizes, g_loc, g_inp, g_plane, g_line, g_out, g_send, g_recv)
    csum = Total(sizes, c_loc, c_inp, c_plane, c_line, c_out, c_send, c_recv)
    ix, iy, iz = lax.axis_index("gx"), lax.axis_index("gy"), lax.axis_index("gz")
    load_w = pltpu.make_async_copy(start_hbm, main.at[pl.ds(1, NRHS), pl.ds(4, 8)], load_sem.at[0])
    load_d = pltpu.make_async_copy(diag_hbm, main.at[0, pl.ds(4, 8)], load_sem.at[1])
    load_h = pltpu.make_async_copy(hist_hbm, hbuf, load_sem.at[2])
    load_w.start()
    load_d.start()
    load_h.start()

    barrier = pltpu.get_barrier_semaphore()
    greeted = [device for _, _, device, _ in gsum.plane_copies()]
    greeted += [device for _, _, device, _ in gsum.line_copies()]
    greeted += [{"gx": lax.rem(ix + 1, nx)}, {"gx": lax.rem(ix + nx - 1, nx)}]
    for dy in (1, ny - 1):
        for dz in (1, nz - 1):
            greeted.append({"gy": lax.rem(iy + dy, ny), "gz": lax.rem(iz + dz, nz)})

    low_x, high_x = ix == 0, ix == nx - 1
    low_y, high_y = iy == 0, iy == ny - 1
    low_z, high_z = iz == 0, iz == nz - 1
    places = 1 + NRHS
    zero = jnp.zeros((places, 8, 128), F32)
    half = jnp.zeros((places, 4, 128), F32)
    side[0:places, 0] = zero
    side[0:places, 15] = zero
    for at, outside in ((0, low_x), (1, high_x)):
        @pl.when(outside)
        def _():
            x_recv[at] = zero
    for at, outside in ((0, low_y), (1, high_y)):
        rows = pl.ds(4 - 4 * at, 4)

        @pl.when(outside)
        def _():
            for z in range(1, 15):
                side[0:places, z, rows] = half
            for third in range(3):
                k_recv[third, :, rows] = half
    for at, outside in ((0, low_z), (1, high_z)):
        @pl.when(outside)
        def _():
            e_recv[at] = zero
            k_recv[1 + at] = zero
            for z in range(12 * at, 12 * at + 4):
                main[0:places, z] = zero
                side[0:places, z] = zero

    for device in greeted:
        pl.semaphore_signal(barrier, inc=1, device_id=device, device_id_type=MESH)

    lane = iota((8, 128), 1)
    row = iota((8, 128), 0)

    def there(dx, dy, dz):
        out = jnp.bool_(True)
        for step, me, count in ((dx, ix, nx), (dy, iy, ny), (dz, iz, nz)):
            if step:
                out = jnp.logical_and(out, me + step >= 0 if step < 0 else me + step < count)
        return out

    def message(number, dx, dy, dz, src, dst):
        device = {}
        for axis, step, me, count in (("gx", dx, ix, nx), ("gy", dy, iy, ny), ("gz", dz, iz, nz)):
            if step:
                device[axis] = lax.rem(me + step + count, count)
        copy = pltpu.make_async_remote_copy(
            src_ref=src, dst_ref=dst, send_sem=hs_sem.at[number], recv_sem=hr_sem.at[number],
            device_id=device, device_id_type=MESH,
        )
        return there(dx, dy, dz), there(-dx, -dy, -dz), copy

    few = pl.ds(0, places)
    rows_of = {1: pl.ds(4, 4), -1: pl.ds(0, 4)}
    first = [message(0, 1, 0, 0, x_send, x_recv.at[0]), message(1, -1, 0, 0, x_send, x_recv.at[1])]
    first.append(message(2, 0, 0, 1, main.at[few, pl.ds(8, 4)], main.at[few, pl.ds(0, 4)]))
    first.append(message(3, 0, 0, -1, main.at[few, pl.ds(4, 4)], main.at[few, pl.ds(12, 4)]))
    second = [message(4, 0, 0, 1, x_own, e_recv.at[0]), message(5, 0, 0, -1, x_own, e_recv.at[1])]
    for k, dy in enumerate((1, -1)):
        rows = rows_of[dy]
        first.append(message(
            6 + k, 0, dy, 0, main.at[few, pl.ds(4, 8), rows], side.at[few, pl.ds(4, 8), rows]))
        second.append(message(8 + k, 0, dy, 0, x_own.at[:, rows], k_recv.at[0, :, rows]))
        for n, dz in enumerate((1, -1)):
            src = pl.ds(9 if dz > 0 else 4, 3)
            dst = pl.ds(1 if dz > 0 else 12, 3)
            first.append(message(
                10 + 2 * k + n, 0, dy, dz, main.at[few, src, rows], side.at[few, dst, rows]))
            second.append(message(14 + 2 * k + n, 0, dy, dz, x_own.at[:, rows], k_recv.at[1 + n, :, rows]))

    def send(messages):
        for sends, _, copy in messages:
            @pl.when(sends)
            def _():
                copy.start()

    def receive(messages):
        for _, comes, copy in messages:
            @pl.when(comes)
            def _():
                copy.wait_recv()

    def leave(messages):
        for sends, _, copy in messages:
            @pl.when(sends)
            def _():
                copy.wait_send()

    def keep_split(level):
        for z in range(8):
            block = main[1 + NRHS * level:1 + NRHS * (level + 1), 4 + z].reshape(8 * NRHS, 128)
            top, low = split(block)
            rows = pl.ds(8 * (HIST + NRHS * level), 8 * NRHS)
            xcat[rows, 128 * z:128 * (z + 1)] = top
            xcat[rows, 1024 + 128 * z:1024 + 128 * (z + 1)] = low

    def turn(value, by, axis):
        by = by % value.shape[axis]
        return value if by == 0 else pltpu.roll(value, by, axis)

    inside = lambda outside: jnp.where(outside, 0.0, 1.0).astype(F32)
    in_z = [inside(low_z) if z < 4 else (inside(high_z) if z > 11 else 1.0) for z in range(16)]
    in_y = jnp.where(row < 4, inside(high_y), inside(low_y))
    in_x = jnp.where(lane % 8 < 4, inside(high_x), inside(low_x))
    in_x = in_x * jnp.where((lane >= 28) & (lane < 92), 1.0, jnp.where((lane >= 92) & (lane < 124), in_z[12], in_z[0]))
    seventh = 1.0 / 7.0

    def beside_x(value, turned):
        at = iota(value.shape, 2)
        left = turn(jnp.where(at == 127, turned, value), 1, 2)
        return left + turn(jnp.where(at == 0, turned, value), -1, 2)

    def beside_y(inner, outer):
        at = iota(inner.shape, inner.ndim - 2)
        inner_low, outer_low = turn(inner, 1, inner.ndim - 2), turn(outer, 1, inner.ndim - 2)
        inner_high, outer_high = turn(inner, -1, inner.ndim - 2), turn(outer, -1, inner.ndim - 2)
        return (
            jnp.where(at == 0, outer_low, inner_low) + jnp.where(at == 7, outer_high, inner_high),
            jnp.where(at == 0, inner_low, outer_low) + jnp.where(at == 7, inner_high, outer_high),
        )

    def beside_edge(value, ends):
        left = jnp.where(lane % 8 == 0, turn(ends, 1, 1), turn(value, 1, 1))
        right = jnp.where(lane % 8 == 7, turn(ends, -1, 1), turn(value, -1, 1))
        return left + right + turn(value, 8, 1) + turn(value, -8, 1)

    def spread(value, low, high):
        return jnp.concatenate([turn(value, -8 * z, 1)[None] for z in range(low, high)], axis=0)

    def ends_of(base, value, low, high):
        turned = [turn(value[z - low], 8 * z, 1) for z in range(low, high)]
        for z in range(low, high):
            base = jnp.where((lane == 8 * z) | (lane == (8 * z + 127) % 128), turned[z - low], base)
        return base

    def advance(level):
        more = level < STEPS - 1
        low, high = level + 1, 15 - level

        def vector(f, carry):
            at = 1 + NRHS * level + f

            def follow(scaled, ref, *place):
                if level > 0:
                    scaled = 2.0 * scaled - ref[(at - NRHS, *place)]
                ref[(at + NRHS, *place)] = scaled

            v, u = main[at, low:high], side[at, low:high]
            edge_v, corner_v = edge[at], corner[at]
            turned = spread(edge_v, low, high)
            if more:
                turned_u = spread(corner_v, low + 1, high - 1)
                ends = ends_of(edge_v, v, low, high)
                side_ends = ends_of(corner_v, u, low, high)
            across = beside_x(v, turned)
            if more:
                across_u = beside_x(u[1:-1], turned_u)
            near, far = beside_y(v, u)
            near = near + across + main[at, low - 1:high - 1] + main[at, low + 1:high + 1]
            follow(main[0, low:high] * v - near * weight_main[low:high], main, slice(low, high))
            if more:
                far = far[1:-1] + across_u + side[at, low:high - 2] + side[at, low + 2:high]
                follow(
                    side[0, low + 1:high - 1] * u[1:-1] - far * weight_side[low + 1:high - 1],
                    side, slice(low + 1, high - 1),
                )
                near, far = beside_y(edge_v, corner_v)
                near = near + beside_edge(edge_v, ends)
                far = far + beside_edge(corner_v, side_ends)
                follow(edge[0] * edge_v - near * (in_x * seventh), edge)
                follow(corner[0] * corner_v - far * (in_x * in_y * seventh), corner)
            return carry

        lax.fori_loop(0, NRHS, vector, 0)

    load_w.wait()
    load_d.wait()
    for place in range(places):
        packed = jnp.zeros((8, 128), F32)
        for z in range(4, 12):
            here = (lane >= 8 * z - 4) & (lane < 8 * z + 4)
            packed = jnp.where(here, turn(main[place, z], 8 * z, 1), packed)
        x_send[place] = packed
    pl.semaphore_wait(barrier, len(greeted))
    send(first)

    load_h.wait()
    for z in range(8):
        top, low = split(hbuf[:, z].reshape(8 * HIST, 128))
        xcat[0:8 * HIST, 128 * z:128 * (z + 1)] = top
        xcat[0:8 * HIST, 1024 + 128 * z:1024 + 128 * (z + 1)] = low
    receive(first[:2])
    for place in range(places):
        x_own[place] = jnp.where(lane % 8 >= 4, x_recv[0, place], x_recv[1, place])
    send(second)
    top, low = xcat[0:8 * HIST, 0:1024], xcat[0:8 * HIST, 1024:2048]
    pairs = bdot(top, top, NT) + bdot(top, low, NT) + bdot(low, top, NT)
    g_loc[0], g_loc[1] = fold_history(pairs)
    gsum.start_pair()
    keep_split(0)

    receive(first[2:])
    receive(second)
    leave(first)
    own = (lane >= 28) & (lane < 92)
    for place in range(places):
        above = turn(jnp.where(lane < 60, e_recv[1, place], e_recv[0, place]), 64, 1)
        edge[place] = jnp.where(own, x_own[place], above)
        above = turn(jnp.where(lane < 60, k_recv[2, place], k_recv[1, place]), 64, 1)
        corner[place] = jnp.where(own, k_recv[0, place], above)
    for z in range(1, 15):
        scaled = (main[0, z] - 1.0) * seventh
        main[0, z] = scaled if 4 <= z < 12 else scaled * in_z[z]
        scaled = (side[0, z] - 1.0) * (in_y * seventh)
        side[0, z] = scaled if 4 <= z < 12 else scaled * in_z[z]
    edge[0] = (edge[0] - 1.0) * (in_x * seventh)
    corner[0] = (corner[0] - 1.0) * (in_x * in_y * seventh)
    for z in range(16):
        weight_main[z] = jnp.full((8, 128), seventh * in_z[z], F32)
        weight_side[z] = in_y * (seventh * in_z[z])
    for level in range(STEPS):
        advance(level)
        keep_split(level + 1)
    gsum.start_plane()
    store = pltpu.make_async_copy(xcat, kept, load_sem.at[0])
    store.start()

    wt = xcat[8 * HIST:8 * (HIST + COLS), 0:1024]
    wl = xcat[8 * HIST:8 * (HIST + COLS), 1024:2048]
    xt, xl = xcat[:, 0:1024], xcat[:, 1024:2048]
    pairs = bdot(xt, wt, NT) + bdot(xt, wl, NT) + bdot(xl, wt, NT)
    c_loc[0], c_loc[1] = fold_basis(pairs)
    csum.start_pair()
    csum.start_plane()
    gsum.start_line()
    leave(second)
    csum.start_line()
    gsum.start_share()
    store.wait()
    sums[2], sums[3] = gsum.result()
    gsum.finish()
    csum.start_share()
    sums[0], sums[1] = csum.result()
    csum.finish()


def finish_kernel(cells, kept, sums_hbm, new_basis, r_out, xcat, sums, done, r_factor, load_sem, store_sem):
    load_sums = pltpu.make_async_copy(sums_hbm, sums, load_sem.at[1])
    load_sums.start()
    load = pltpu.make_async_copy(kept, xcat, load_sem.at[0])
    load.start()
    load_sums.wait()
    scale = 1.0 / cells
    one, two, three, four = [sums[k] * scale for k in range(4)]
    gram_h, right_h = unfold_history([three, four])
    lane = iota((24, 128), 1)
    row = iota((24, 128), 0)
    coef, own = unfold_basis(one, two)
    work = fdot(coef[:, 0:HIST], gram_h, NN) + fdot(coef, jnp.concatenate([right_h, jnp.zeros((72, 128), F32)], axis=0), NT)
    wide = jnp.concatenate([coef, jnp.zeros((104, 128), F32)], axis=0)
    gram = fdot(work - 2.0 * coef, wide, NT) + own
    rhs = jnp.where(lane < HIST, -coef, jnp.where(lane - HIST == row, 1.0, 0.0))

    columns = [jnp.broadcast_to(gram[:, k:k + 1], (24, 128)) for k in range(COLS)]
    lower = jnp.zeros((24, 128), F32)
    for j in range(COLS):
        pivot = jnp.broadcast_to(columns[j][j:j + 1], (24, 128))
        inverse = lax.rsqrt(pivot)
        inverse = inverse * (1.5 - 0.5 * pivot * inverse * inverse)
        column = jnp.where(row >= j, columns[j] * inverse, 0.0)
        lower = jnp.where(lane == j, column, lower)
        solved = jnp.broadcast_to(rhs[j:j + 1], (24, 128)) * inverse
        rhs = jnp.where(row == j, solved, rhs - jnp.where(row > j, column * solved, 0.0))
        for k in range(j + 1, COLS):
            columns[k] = columns[k] - column * jnp.broadcast_to(column[k:k + 1], (24, 128))
    square = jnp.concatenate([lower, jnp.zeros((104, 128), F32)], axis=0)
    r_factor[...] = square.T[0:COLS, 0:COLS]
    store_r = pltpu.make_async_copy(r_factor, r_out, store_sem.at[4])
    store_r.start()

    weights = rhs[0:COLS]
    top, low = split(weights)
    spread = ((iota((128, 8 * (HIST + COLS)), 1) // 8) == iota((128, 8 * (HIST + COLS)), 0)).astype(BF16)
    size = (8 * COLS, 8 * (HIST + COLS))
    same = (iota(size, 0) % 8) == (iota(size, 1) % 8)

    def widen(part):
        wide = bdot(part, spread, NN)
        wide = jnp.broadcast_to(wide[:, None, :], (COLS, 8, size[1])).reshape(size)
        return jnp.where(same, wide, 0.0).astype(BF16)

    top, low = widen(top), widen(low)
    load.wait()
    stores = []
    for part in range(4):
        cols = slice(256 * part, 256 * (part + 1))
        lows = slice(1024 + 256 * part, 1024 + 256 * (part + 1))
        out = bdot(top, xcat[:, cols], NN) + bdot(top, xcat[:, lows], NN) + bdot(low, xcat[:, cols], NN)
        for half in range(2):
            done[:, 2 * part + half] = out[:, 128 * half:128 * (half + 1)].reshape(COLS, 8, 128)
        layers = pl.ds(2 * part, 2)
        stores.append(pltpu.make_async_copy(done.at[:, layers], new_basis.at[:, layers], store_sem.at[part]))
        stores[-1].start()
    for copy in stores:
        copy.wait()
    store_r.wait()


def on_device(nx, ny, nz, history, start, diagonal):
    dma = pltpu.SemaphoreType.DMA
    tiles = lambda *shape: pltpu.VMEM((*shape, 8, 128), F32)
    plane = (nx // 2) * nz
    reduction = [tiles(2), tiles(), tiles(plane), tiles(ny), tiles(2)]
    any_spec = pl.BlockSpec(memory_space=pl.ANY)
    vmem = pl.BlockSpec(memory_space=pltpu.VMEM)
    cells = float(nx * ny * nz * diagonal.size)
    kept, sums = pl.pallas_call(
        functools.partial(cycle_kernel, nx, ny, nz),
        name="cycle",
        out_shape=(
            jax.ShapeDtypeStruct((8 * (HIST + COLS), 2048), BF16),
            jax.ShapeDtypeStruct((4, 8, 128), F32),
        ),
        in_specs=[any_spec] * 3,
        out_specs=(any_spec, vmem),
        scratch_shapes=[
            pltpu.VMEM((8 * (HIST + COLS), 2048), BF16),
            tiles(HIST, 8),
            tiles(1 + COLS, 16),
            tiles(1 + NRHS * STEPS, 16),
            tiles(1 + NRHS * STEPS),
            tiles(1 + NRHS * STEPS),
            tiles(1 + NRHS),
            tiles(2, 1 + NRHS),
            tiles(1 + NRHS),
            tiles(2, 1 + NRHS),
            tiles(3, 1 + NRHS),
            tiles(16),
            tiles(16),
            *reduction,
            *reduction,
            dma((3,)), dma((18,)), dma((18,)),
            *[dma((2 + plane + ny,))] * 4,
        ],
        compiler_params=pltpu.CompilerParams(
            collective_id=0, has_side_effects=True, vmem_limit_bytes=VMEM_BYTES
        ),
    )(history, start, diagonal)
    return pl.pallas_call(
        functools.partial(finish_kernel, cells),
        name="finish",
        out_shape=(
            jax.ShapeDtypeStruct((COLS, 8, 8, 128), F32),
            jax.ShapeDtypeStruct((COLS, COLS), F32),
        ),
        in_specs=[any_spec, any_spec],
        out_specs=(any_spec, any_spec),
        scratch_shapes=[
            pltpu.VMEM((8 * (HIST + COLS), 2048), BF16),
            tiles(4),
            tiles(COLS, 8),
            pltpu.VMEM((COLS, COLS), F32),
            dma((2,)),
            dma((5,)),
        ],
        compiler_params=pltpu.CompilerParams(vmem_limit_bytes=VMEM_BYTES),
    )(kept, sums)


def solution(mesh):
    return jax.shard_map(
        functools.partial(on_device, mesh.shape["gx"], mesh.shape["gy"], mesh.shape["gz"]),
        mesh=mesh,
        in_specs=(P(None, "gz", "gy", "gx"), P(None, "gz", "gy", "gx"), P("gz", "gy", "gx")),
        out_specs=(P(None, "gz", "gy", "gx"), P()),
        check_vma=False,
    )
```

```python
import functools

import jax
import jax.numpy as jnp
from jax import lax
from jax.experimental import pallas as pl
from jax.experimental.pallas import tpu as pltpu
from jax.sharding import PartitionSpec as P

STEPS = 4
NRHS = 4
HIST = 56
COLS = 20
MESH = pl.DeviceIdType.MESH
F32 = jnp.float32
BF16 = jnp.bfloat16
NT = (((1,), (1,)), ((), ()))
NN = (((1,), (0,)), ((), ()))
HIGH = lax.Precision.HIGHEST
VMEM_BYTES = 66_300_000


def iota(shape, dim):
    return lax.broadcasted_iota(jnp.int32, shape, dim)


def split(value):
    top = value.astype(BF16)
    return top, (value - top.astype(F32)).astype(BF16)


def bdot(left, right, dims):
    return lax.dot_general(left, right, dims, preferred_element_type=F32)


def fdot(left, right, dims):
    return lax.dot_general(left, right, dims, precision=HIGH, preferred_element_type=F32)


def keep_same_row(value):
    same = (iota(value.shape, 0) % 8) == (iota(value.shape, 1) % 8)
    masked = jnp.where(same, value, 0.0)
    return jnp.sum(masked.reshape(value.shape[0] // 8, 8, value.shape[1]), axis=1)


def thirds(value):
    first = value.astype(BF16)
    rest = value - first.astype(F32)
    second = rest.astype(BF16)
    return first, second, (rest - second.astype(F32)).astype(BF16)


class Total:
    def __init__(self, sizes, loc, inp, plane, line, out, send, recv):
        self.nx, self.ny, self.nz = sizes
        self.loc, self.inp, self.plane, self.line, self.out = loc, inp, plane, line, out
        self.send, self.recv = send, recv
        self.ix, self.iy, self.iz = lax.axis_index("gx"), lax.axis_index("gy"), lax.axis_index("gz")
        self.core = lax.rem(self.ix, 2)
        self.iyc = self.ix // 2

    def pair_copy(self, src, dst, number):
        return pltpu.make_async_remote_copy(
            src_ref=src, dst_ref=dst, send_sem=self.send.at[number], recv_sem=self.recv.at[number],
            device_id={"gx": self.ix + 1 - 2 * self.core}, device_id_type=MESH,
        )

    def plane_copies(self):
        nyc, nz = self.nx // 2, self.nz
        for step in range(1, nyc * nz):
            py = lax.rem(self.iyc + step // nz, nyc)
            pz = lax.rem(self.iz + step % nz, nz)
            yield py * nz + pz, self.iyc * nz + self.iz, {"gx": 2 * py + self.core, "gz": pz}, 2 + step

    def line_copies(self):
        for step in range(1, self.ny):
            peer = lax.rem(self.iy + step, self.ny)
            yield peer, self.iy, {"gy": peer}, 2 + (self.nx // 2) * self.nz + step

    def spread(self, copies, buf, base):
        for peer, me, device, number in copies:
            pltpu.make_async_remote_copy(
                src_ref=buf.at[me], dst_ref=buf.at[me], send_sem=self.send.at[number],
                recv_sem=self.recv.at[base + me], device_id=device, device_id_type=MESH,
            ).start()

    def collect(self, copies, buf, base):
        for peer, _, device, number in copies:
            pltpu.make_async_remote_copy(
                src_ref=buf.at[peer], dst_ref=buf.at[peer], send_sem=self.send.at[number],
                recv_sem=self.recv.at[base + peer], device_id=device, device_id_type=MESH,
            ).wait_recv()

    def drain(self, copies, buf, base):
        for peer, me, device, number in copies:
            pltpu.make_async_remote_copy(
                src_ref=buf.at[me], dst_ref=buf.at[me], send_sem=self.send.at[number],
                recv_sem=self.recv.at[base + me], device_id=device, device_id_type=MESH,
            ).wait_send()

    def first(self):
        return self.pair_copy(self.loc.at[1 - self.core], self.inp, 0)

    def last(self):
        return self.pair_copy(self.out.at[self.core], self.out.at[self.core], 1)

    def start_pair(self):
        self.first().start()

    def start_plane(self):
        self.first().wait_recv()
        self.plane[self.iyc * self.nz + self.iz] = self.loc[self.core] + self.inp[...]
        self.spread(self.plane_copies(), self.plane, 2)

    def start_line(self):
        self.collect(self.plane_copies(), self.plane, 2)
        self.line[self.iy] = total_of(self.plane)
        self.spread(self.line_copies(), self.line, 2 + (self.nx // 2) * self.nz)

    def start_share(self):
        self.collect(self.line_copies(), self.line, 2 + (self.nx // 2) * self.nz)
        self.out[self.core] = total_of(self.line)
        self.last().start()

    def result(self):
        other = self.out.at[1 - self.core]
        self.pair_copy(other, other, 1).wait_recv()
        return self.out[0], self.out[1]

    def finish(self):
        self.first().wait_send()
        self.drain(self.plane_copies(), self.plane, 2)
        self.drain(self.line_copies(), self.line, 2 + (self.nx // 2) * self.nz)


def total_of(ref):
    parts = [ref[place] for place in range(ref.shape[0])]
    while len(parts) > 1:
        parts = [sum(parts[k:k + 2][1:], parts[k]) for k in range(0, len(parts), 2)]
    return parts[0]


def fold_history(pairs):
    rows = jnp.concatenate(thirds(keep_same_row(pairs)), axis=0)
    pick = ((iota((8 * HIST, 128), 0) // 8) == iota((8 * HIST, 128), 1)).astype(BF16)
    parts = bdot(rows, pick, NN)
    full = parts[0:HIST] + parts[HIST:2 * HIST] + parts[2 * HIST:3 * HIST]
    lane = iota((8, 128), 1)
    tiles = []
    for half in range(2):
        low = 8 * half
        tile = jnp.where(lane < 56, full[low:low + 8], 0.0)
        tile = jnp.where((lane >= 56) & (lane < 96), pltpu.roll(full[16 + low:24 + low], 40, 1), tile)
        tile = jnp.where((lane >= 96) & (lane < 120), pltpu.roll(full[32 + low:40 + low], 64, 1), tile)
        if half == 0:
            tile = jnp.where(lane >= 120, pltpu.roll(full[48:56], 72, 1), tile)
        tiles.append(tile)
    return tiles


def unfold_history(tiles):
    lane = iota((8, 128), 1)
    rows = []
    for first, turn in ((0, 0), (16, 88), (32, 64), (48, 56)):
        for tile in tiles[:1] if first == 48 else tiles:
            turned = tile if turn == 0 else pltpu.roll(tile, turn, 1)
            rows.append(jnp.where((lane >= first) & (lane < HIST), turned, 0.0))
    upper = jnp.concatenate(rows, axis=0)
    right = jnp.where(iota((HIST, 128), 1) >= 16 * (iota((HIST, 128), 0) // 16) + 16, upper, 0.0)
    return upper, right


def fold_basis(pairs):
    rows = keep_same_row(pairs)
    rows = jnp.concatenate([rows, jnp.zeros((128 - HIST - COLS, 8 * COLS), F32)], axis=0)
    rows = jnp.concatenate(thirds(rows), axis=0)
    pick = (iota((24, 8 * COLS), 0) == (iota((24, 8 * COLS), 1) // 8)).astype(BF16)
    parts = bdot(pick, rows, NT)
    full = parts[:, 0:128] + parts[:, 128:256] + parts[:, 256:384]
    lane = iota((8, 128), 1)
    one = jnp.where(lane < HIST, full[0:8], jnp.where(lane >= 64, pltpu.roll(full[8:16], 64, 1), 0.0))
    two = jnp.where(lane < HIST, full[16:24], 0.0)
    for part in range(3):
        first = 64 + 20 * part
        turned = pltpu.roll(full[8 * part:8 * part + 8], first - HIST, 1)
        two = jnp.where((lane >= first) & (lane < first + COLS), turned, two)
    return one, two


def unfold_basis(one, two):
    lane = iota((24, 128), 1)
    coef = jnp.concatenate([one, pltpu.roll(one, 64, 1), two], axis=0)
    own = jnp.concatenate([pltpu.roll(two, 128 - 64 - 20 * part, 1) for part in range(3)], axis=0)
    return jnp.where(lane < HIST, coef, 0.0), jnp.where(lane < COLS, own, 0.0)


def cycle_kernel(
    nx, ny, nz,
    hist_hbm, start_hbm, diag_hbm,
    kept, sums,
    xcat, hbuf, main, side, edge, corner, x_send, x_recv, x_own, e_recv, k_recv, weight_main, weight_side,
    g_loc, g_inp, g_plane, g_line, g_out,
    c_loc, c_inp, c_plane, c_line, c_out,
    load_sem, heard, hs_sem, hr_sem, g_send, g_recv, c_send, c_recv,
):
    sizes = (nx, ny, nz)
    gsum = Total(sizes, g_loc, g_inp, g_plane, g_line, g_out, g_send, g_recv)
    csum = Total(sizes, c_loc, c_inp, c_plane, c_line, c_out, c_send, c_recv)
    ix, iy, iz = lax.axis_index("gx"), lax.axis_index("gy"), lax.axis_index("gz")
    load_w = pltpu.make_async_copy(start_hbm, main.at[pl.ds(1, NRHS), pl.ds(4, 8)], load_sem.at[0])
    load_d = pltpu.make_async_copy(diag_hbm, main.at[0, pl.ds(4, 8)], load_sem.at[1])
    load_h = pltpu.make_async_copy(hist_hbm, hbuf, load_sem.at[2])
    load_w.start()
    load_d.start()
    load_h.start()

    barrier = pltpu.get_barrier_semaphore()
    greeted = [device for _, _, device, _ in gsum.plane_copies()]
    reach = max(1, ny // 4)
    for step in range(1, reach + 1):
        greeted += [{"gy": lax.rem(iy + step, ny)}, {"gy": lax.rem(iy + ny - step, ny)}]
    greeted += [{"gx": lax.rem(ix + 1, nx)}, {"gx": lax.rem(ix + nx - 1, nx)}]
    for dy in (1, ny - 1):
        for dz in (1, nz - 1):
            greeted.append({"gy": lax.rem(iy + dy, ny), "gz": lax.rem(iz + dz, nz)})

    low_x, high_x = ix == 0, ix == nx - 1
    low_y, high_y = iy == 0, iy == ny - 1
    low_z, high_z = iz == 0, iz == nz - 1
    places = 1 + NRHS
    zero = jnp.zeros((places, 8, 128), F32)
    half = jnp.zeros((places, 4, 128), F32)
    side[0:places, 0] = zero
    side[0:places, 15] = zero
    for at, outside in ((0, low_x), (1, high_x)):
        @pl.when(outside)
        def _():
            x_recv[at] = zero
    for at, outside in ((0, low_y), (1, high_y)):
        rows = pl.ds(4 - 4 * at, 4)

        @pl.when(outside)
        def _():
            for z in range(1, 15):
                side[0:places, z, rows] = half
            for third in range(3):
                k_recv[third, :, rows] = half
    for at, outside in ((0, low_z), (1, high_z)):
        @pl.when(outside)
        def _():
            e_recv[at] = zero
            k_recv[1 + at] = zero
            for z in range(12 * at, 12 * at + 4):
                main[0:places, z] = zero
                side[0:places, z] = zero

    for device in greeted:
        pl.semaphore_signal(barrier, inc=1, device_id=device, device_id_type=MESH)

    lane = iota((8, 128), 1)
    row = iota((8, 128), 0)

    def there(dx, dy, dz):
        out = jnp.bool_(True)
        for step, me, count in ((dx, ix, nx), (dy, iy, ny), (dz, iz, nz)):
            if step:
                out = jnp.logical_and(out, me + step >= 0 if step < 0 else me + step < count)
        return out

    def message(number, dx, dy, dz, src, dst):
        device = {}
        for axis, step, me, count in (("gx", dx, ix, nx), ("gy", dy, iy, ny), ("gz", dz, iz, nz)):
            if step:
                device[axis] = lax.rem(me + step + count, count)
        copy = pltpu.make_async_remote_copy(
            src_ref=src, dst_ref=dst, send_sem=hs_sem.at[number], recv_sem=hr_sem.at[number],
            device_id=device, device_id_type=MESH,
        )
        return there(dx, dy, dz), there(-dx, -dy, -dz), copy

    few = pl.ds(0, places)
    rows_of = {1: pl.ds(4, 4), -1: pl.ds(0, 4)}
    first = [message(0, 1, 0, 0, x_send, x_recv.at[0]), message(1, -1, 0, 0, x_send, x_recv.at[1])]
    first.append(message(2, 0, 0, 1, main.at[few, pl.ds(8, 4)], main.at[few, pl.ds(0, 4)]))
    first.append(message(3, 0, 0, -1, main.at[few, pl.ds(4, 4)], main.at[few, pl.ds(12, 4)]))
    second = [message(4, 0, 0, 1, x_own, e_recv.at[0]), message(5, 0, 0, -1, x_own, e_recv.at[1])]
    for k, dy in enumerate((1, -1)):
        rows = rows_of[dy]
        first.append(message(
            6 + k, 0, dy, 0, main.at[few, pl.ds(4, 8), rows], side.at[few, pl.ds(4, 8), rows]))
        second.append(message(8 + k, 0, dy, 0, x_own.at[:, rows], k_recv.at[0, :, rows]))
        for n, dz in enumerate((1, -1)):
            src = pl.ds(9 if dz > 0 else 4, 3)
            dst = pl.ds(1 if dz > 0 else 12, 3)
            first.append(message(
                10 + 2 * k + n, 0, dy, dz, main.at[few, src, rows], side.at[few, dst, rows]))
            second.append(message(14 + 2 * k + n, 0, dy, dz, x_own.at[:, rows], k_recv.at[1 + n, :, rows]))

    def send(messages):
        for sends, _, copy in messages:
            @pl.when(sends)
            def _():
                copy.start()

    def receive(messages):
        for _, comes, copy in messages:
            @pl.when(comes)
            def _():
                copy.wait_recv()

    def leave(messages):
        for sends, _, copy in messages:
            @pl.when(sends)
            def _():
                copy.wait_send()

    def keep_split(level):
        for z in range(8):
            block = main[1 + NRHS * level:1 + NRHS * (level + 1), 4 + z].reshape(8 * NRHS, 128)
            top, low = split(block)
            rows = pl.ds(8 * (HIST + NRHS * level), 8 * NRHS)
            xcat[rows, 128 * z:128 * (z + 1)] = top
            xcat[rows, 1024 + 128 * z:1024 + 128 * (z + 1)] = low

    def turn(value, by, axis):
        by = by % value.shape[axis]
        return value if by == 0 else pltpu.roll(value, by, axis)

    inside = lambda outside: jnp.where(outside, 0.0, 1.0).astype(F32)
    in_z = [inside(low_z) if z < 4 else (inside(high_z) if z > 11 else 1.0) for z in range(16)]
    in_y = jnp.where(row < 4, inside(high_y), inside(low_y))
    in_x = jnp.where(lane % 8 < 4, inside(high_x), inside(low_x))
    in_x = in_x * jnp.where((lane >= 28) & (lane < 92), 1.0, jnp.where((lane >= 92) & (lane < 124), in_z[12], in_z[0]))
    seventh = 1.0 / 7.0

    def beside_x(value, turned):
        at = iota(value.shape, 2)
        left = turn(jnp.where(at == 127, turned, value), 1, 2)
        return left + turn(jnp.where(at == 0, turned, value), -1, 2)

    def beside_y(inner, outer):
        at = iota(inner.shape, inner.ndim - 2)
        inner_low, outer_low = turn(inner, 1, inner.ndim - 2), turn(outer, 1, inner.ndim - 2)
        inner_high, outer_high = turn(inner, -1, inner.ndim - 2), turn(outer, -1, inner.ndim - 2)
        return (
            jnp.where(at == 0, outer_low, inner_low) + jnp.where(at == 7, outer_high, inner_high),
            jnp.where(at == 0, inner_low, outer_low) + jnp.where(at == 7, inner_high, outer_high),
        )

    def beside_edge(value, ends):
        left = jnp.where(lane % 8 == 0, turn(ends, 1, 1), turn(value, 1, 1))
        right = jnp.where(lane % 8 == 7, turn(ends, -1, 1), turn(value, -1, 1))
        return left + right + turn(value, 8, 1) + turn(value, -8, 1)

    def spread(value, low, high):
        return jnp.concatenate([turn(value, -8 * z, 1)[None] for z in range(low, high)], axis=0)

    def ends_of(base, value, low, high):
        turned = [turn(value[z - low], 8 * z, 1) for z in range(low, high)]
        for z in range(low, high):
            base = jnp.where((lane == 8 * z) | (lane == (8 * z + 127) % 128), turned[z - low], base)
        return base

    def advance(level):
        more = level < STEPS - 1
        low, high = level + 1, 15 - level

        def vector(f, carry):
            at = 1 + NRHS * level + f

            def follow(scaled, ref, *place):
                if level > 0:
                    scaled = 2.0 * scaled - ref[(at - NRHS, *place)]
                ref[(at + NRHS, *place)] = scaled

            v, u = main[at, low:high], side[at, low:high]
            edge_v, corner_v = edge[at], corner[at]
            turned = spread(edge_v, low, high)
            if more:
                turned_u = spread(corner_v, low + 1, high - 1)
                ends = ends_of(edge_v, v, low, high)
                side_ends = ends_of(corner_v, u, low, high)
            across = beside_x(v, turned)
            if more:
                across_u = beside_x(u[1:-1], turned_u)
            near, far = beside_y(v, u)
            near = near + across + main[at, low - 1:high - 1] + main[at, low + 1:high + 1]
            follow(main[0, low:high] * v - near * weight_main[low:high], main, slice(low, high))
            if more:
                far = far[1:-1] + across_u + side[at, low:high - 2] + side[at, low + 2:high]
                follow(
                    side[0, low + 1:high - 1] * u[1:-1] - far * weight_side[low + 1:high - 1],
                    side, slice(low + 1, high - 1),
                )
                near, far = beside_y(edge_v, corner_v)
                near = near + beside_edge(edge_v, ends)
                far = far + beside_edge(corner_v, side_ends)
                follow(edge[0] * edge_v - near * (in_x * seventh), edge)
                follow(corner[0] * corner_v - far * (in_x * in_y * seventh), corner)
            return carry

        lax.fori_loop(0, NRHS, vector, 0)

    load_w.wait()
    load_d.wait()
    for place in range(places):
        packed = jnp.zeros((8, 128), F32)
        for z in range(4, 12):
            here = (lane >= 8 * z - 4) & (lane < 8 * z + 4)
            packed = jnp.where(here, turn(main[place, z], 8 * z, 1), packed)
        x_send[place] = packed
    pl.semaphore_wait(barrier, len(greeted))
    send(first)
    for side_of, step in ((0, reach), (1, ny - reach)):
        pl.semaphore_signal(
            heard.at[side_of], inc=1, device_id={"gy": lax.rem(iy + step, ny)}, device_id_type=MESH
        )

    load_h.wait()
    for z in range(8):
        top, low = split(hbuf[:, z].reshape(8 * HIST, 128))
        xcat[0:8 * HIST, 128 * z:128 * (z + 1)] = top
        xcat[0:8 * HIST, 1024 + 128 * z:1024 + 128 * (z + 1)] = low
    receive(first[:2])
    for place in range(places):
        x_own[place] = jnp.where(lane % 8 >= 4, x_recv[0, place], x_recv[1, place])
    send(second)
    top, low = xcat[0:8 * HIST, 0:1024], xcat[0:8 * HIST, 1024:2048]
    pairs = bdot(top, top, NT) + bdot(top, low, NT) + bdot(low, top, NT)
    g_loc[0], g_loc[1] = fold_history(pairs)
    gsum.start_pair()
    keep_split(0)

    receive(first[2:])
    receive(second)
    leave(first)
    own = (lane >= 28) & (lane < 92)
    for place in range(places):
        above = turn(jnp.where(lane < 60, e_recv[1, place], e_recv[0, place]), 64, 1)
        edge[place] = jnp.where(own, x_own[place], above)
        above = turn(jnp.where(lane < 60, k_recv[2, place], k_recv[1, place]), 64, 1)
        corner[place] = jnp.where(own, k_recv[0, place], above)
    for z in range(1, 15):
        scaled = (main[0, z] - 1.0) * seventh
        main[0, z] = scaled if 4 <= z < 12 else scaled * in_z[z]
        scaled = (side[0, z] - 1.0) * (in_y * seventh)
        side[0, z] = scaled if 4 <= z < 12 else scaled * in_z[z]
    edge[0] = (edge[0] - 1.0) * (in_x * seventh)
    corner[0] = (corner[0] - 1.0) * (in_x * in_y * seventh)
    for z in range(16):
        weight_main[z] = jnp.full((8, 128), seventh * in_z[z], F32)
        weight_side[z] = in_y * (seventh * in_z[z])
    for level in range(STEPS):
        advance(level)
        keep_split(level + 1)
    gsum.start_plane()
    store = pltpu.make_async_copy(xcat, kept, load_sem.at[0])
    store.start()

    wt = xcat[8 * HIST:8 * (HIST + COLS), 0:1024]
    wl = xcat[8 * HIST:8 * (HIST + COLS), 1024:2048]
    xt, xl = xcat[:, 0:1024], xcat[:, 1024:2048]
    pairs = bdot(xt, wt, NT) + bdot(xt, wl, NT) + bdot(xl, wt, NT)
    c_loc[0], c_loc[1] = fold_basis(pairs)
    csum.start_pair()
    csum.start_plane()
    for side_of in range(2):
        pl.semaphore_wait(heard.at[side_of], 1)
    gsum.start_line()
    leave(second)
    csum.start_line()
    gsum.start_share()
    store.wait()
    sums[2], sums[3] = gsum.result()
    gsum.finish()
    gsum.last().wait_send()
    csum.start_share()
    csum.finish()
    sums[0], sums[1] = csum.result()
    csum.last().wait_send()


def finish_kernel(cells, kept, sums_hbm, new_basis, r_out, xcat, sums, done, r_factor, load_sem, store_sem):
    load_sums = pltpu.make_async_copy(sums_hbm, sums, load_sem.at[1])
    load_sums.start()
    load = pltpu.make_async_copy(kept, xcat, load_sem.at[0])
    load.start()
    load_sums.wait()
    scale = 1.0 / cells
    one, two, three, four = [sums[k] * scale for k in range(4)]
    gram_h, right_h = unfold_history([three, four])
    lane = iota((24, 128), 1)
    row = iota((24, 128), 0)
    coef, own = unfold_basis(one, two)
    work = fdot(coef[:, 0:HIST], gram_h, NN) + fdot(coef, jnp.concatenate([right_h, jnp.zeros((72, 128), F32)], axis=0), NT)
    wide = jnp.concatenate([coef, jnp.zeros((104, 128), F32)], axis=0)
    gram = fdot(work - 2.0 * coef, wide, NT) + own
    rhs = jnp.where(lane < HIST, -coef, jnp.where(lane - HIST == row, 1.0, 0.0))

    columns = [jnp.broadcast_to(gram[:, k:k + 1], (24, 128)) for k in range(COLS)]
    lower = jnp.zeros((24, 128), F32)
    for j in range(COLS):
        pivot = jnp.broadcast_to(columns[j][j:j + 1], (24, 128))
        inverse = lax.rsqrt(pivot)
        inverse = inverse * (1.5 - 0.5 * pivot * inverse * inverse)
        column = jnp.where(row >= j, columns[j] * inverse, 0.0)
        lower = jnp.where(lane == j, column, lower)
        solved = jnp.broadcast_to(rhs[j:j + 1], (24, 128)) * inverse
        rhs = jnp.where(row == j, solved, rhs - jnp.where(row > j, column * solved, 0.0))
        for k in range(j + 1, COLS):
            columns[k] = columns[k] - column * jnp.broadcast_to(column[k:k + 1], (24, 128))
    square = jnp.concatenate([lower, jnp.zeros((104, 128), F32)], axis=0)
    r_factor[...] = square.T[0:COLS, 0:COLS]
    store_r = pltpu.make_async_copy(r_factor, r_out, store_sem.at[4])
    store_r.start()

    weights = rhs[0:COLS]
    top, low = split(weights)
    spread = ((iota((128, 8 * (HIST + COLS)), 1) // 8) == iota((128, 8 * (HIST + COLS)), 0)).astype(BF16)
    size = (8 * COLS, 8 * (HIST + COLS))
    same = (iota(size, 0) % 8) == (iota(size, 1) % 8)

    def widen(part):
        wide = bdot(part, spread, NN)
        wide = jnp.broadcast_to(wide[:, None, :], (COLS, 8, size[1])).reshape(size)
        return jnp.where(same, wide, 0.0).astype(BF16)

    top, low = widen(top), widen(low)
    load.wait()
    stores = []
    for part in range(4):
        cols = slice(256 * part, 256 * (part + 1))
        lows = slice(1024 + 256 * part, 1024 + 256 * (part + 1))
        out = bdot(top, xcat[:, cols], NN) + bdot(top, xcat[:, lows], NN) + bdot(low, xcat[:, cols], NN)
        for half in range(2):
            done[:, 2 * part + half] = out[:, 128 * half:128 * (half + 1)].reshape(COLS, 8, 128)
        layers = pl.ds(2 * part, 2)
        stores.append(pltpu.make_async_copy(done.at[:, layers], new_basis.at[:, layers], store_sem.at[part]))
        stores[-1].start()
    for copy in stores:
        copy.wait()
    store_r.wait()


def on_device(nx, ny, nz, history, start, diagonal):
    dma = pltpu.SemaphoreType.DMA
    tiles = lambda *shape: pltpu.VMEM((*shape, 8, 128), F32)
    plane = (nx // 2) * nz
    reduction = [tiles(2), tiles(), tiles(plane), tiles(ny), tiles(2)]
    any_spec = pl.BlockSpec(memory_space=pl.ANY)
    vmem = pl.BlockSpec(memory_space=pltpu.VMEM)
    cells = float(nx * ny * nz * diagonal.size)
    kept, sums = pl.pallas_call(
        functools.partial(cycle_kernel, nx, ny, nz),
        name="cycle",
        out_shape=(
            jax.ShapeDtypeStruct((8 * (HIST + COLS), 2048), BF16),
            jax.ShapeDtypeStruct((4, 8, 128), F32),
        ),
        in_specs=[any_spec] * 3,
        out_specs=(any_spec, vmem),
        scratch_shapes=[
            pltpu.VMEM((8 * (HIST + COLS), 2048), BF16),
            tiles(HIST, 8),
            tiles(1 + COLS, 16),
            tiles(1 + NRHS * STEPS, 16),
            tiles(1 + NRHS * STEPS),
            tiles(1 + NRHS * STEPS),
            tiles(1 + NRHS),
            tiles(2, 1 + NRHS),
            tiles(1 + NRHS),
            tiles(2, 1 + NRHS),
            tiles(3, 1 + NRHS),
            tiles(16),
            tiles(16),
            *reduction,
            *reduction,
            dma((3,)), pltpu.SemaphoreType.REGULAR((2,)), dma((18,)), dma((18,)),
            *[dma((2 + plane + ny,))] * 4,
        ],
        compiler_params=pltpu.CompilerParams(
            collective_id=0, has_side_effects=True, vmem_limit_bytes=VMEM_BYTES
        ),
    )(history, start, diagonal)
    return pl.pallas_call(
        functools.partial(finish_kernel, cells),
        name="finish",
        out_shape=(
            jax.ShapeDtypeStruct((COLS, 8, 8, 128), F32),
            jax.ShapeDtypeStruct((COLS, COLS), F32),
        ),
        in_specs=[any_spec, any_spec],
        out_specs=(any_spec, any_spec),
        scratch_shapes=[
            pltpu.VMEM((8 * (HIST + COLS), 2048), BF16),
            tiles(4),
            tiles(COLS, 8),
            pltpu.VMEM((COLS, COLS), F32),
            dma((2,)),
            dma((5,)),
        ],
        compiler_params=pltpu.CompilerParams(vmem_limit_bytes=VMEM_BYTES),
    )(kept, sums)


def solution(mesh):
    return jax.shard_map(
        functools.partial(on_device, mesh.shape["gx"], mesh.shape["gy"], mesh.shape["gz"]),
        mesh=mesh,
        in_specs=(P(None, "gz", "gy", "gx"), P(None, "gz", "gy", "gx"), P("gz", "gy", "gx")),
        out_specs=(P(None, "gz", "gy", "gx"), P()),
        check_vma=False,
    )
```

```python
import functools

import jax
import jax.numpy as jnp
from jax import lax
from jax.experimental import pallas as pl
from jax.experimental.pallas import tpu as pltpu
from jax.sharding import PartitionSpec as P

STEPS = 4
NRHS = 4
HIST = 56
COLS = 20
MESH = pl.DeviceIdType.MESH
F32 = jnp.float32
BF16 = jnp.bfloat16
NT = (((1,), (1,)), ((), ()))
NN = (((1,), (0,)), ((), ()))
HIGH = lax.Precision.HIGHEST
VMEM_BYTES = 56_520_000


def iota(shape, dim):
    return lax.broadcasted_iota(jnp.int32, shape, dim)


def split(value):
    top = value.astype(BF16)
    return top, (value - top.astype(F32)).astype(BF16)


def bdot(left, right, dims):
    return lax.dot_general(left, right, dims, preferred_element_type=F32)


def fdot(left, right, dims):
    return lax.dot_general(left, right, dims, precision=HIGH, preferred_element_type=F32)


def keep_same_row(value):
    same = (iota(value.shape, 0) % 8) == (iota(value.shape, 1) % 8)
    masked = jnp.where(same, value, 0.0)
    return jnp.sum(masked.reshape(value.shape[0] // 8, 8, value.shape[1]), axis=1)


def thirds(value):
    first = value.astype(BF16)
    rest = value - first.astype(F32)
    second = rest.astype(BF16)
    return first, second, (rest - second.astype(F32)).astype(BF16)


class Total:
    def __init__(self, sizes, loc, inp, plane, line, out, send, recv):
        self.nx, self.ny, self.nz = sizes
        self.loc, self.inp, self.plane, self.line, self.out = loc, inp, plane, line, out
        self.send, self.recv = send, recv
        self.ix, self.iy, self.iz = lax.axis_index("gx"), lax.axis_index("gy"), lax.axis_index("gz")
        self.core = lax.rem(self.ix, 2)
        self.iyc = self.ix // 2

    def pair_copy(self, src, dst, number):
        return pltpu.make_async_remote_copy(
            src_ref=src, dst_ref=dst, send_sem=self.send.at[number], recv_sem=self.recv.at[number],
            device_id={"gx": self.ix + 1 - 2 * self.core}, device_id_type=MESH,
        )

    def plane_copies(self):
        nyc, nz = self.nx // 2, self.nz
        for step in range(1, nyc * nz):
            py = lax.rem(self.iyc + step // nz, nyc)
            pz = lax.rem(self.iz + step % nz, nz)
            yield py * nz + pz, self.iyc * nz + self.iz, {"gx": 2 * py + self.core, "gz": pz}, 2 + step

    def line_copies(self):
        for step in range(1, self.ny):
            peer = lax.rem(self.iy + step, self.ny)
            yield peer, self.iy, {"gy": peer}, 2 + (self.nx // 2) * self.nz + step

    def spread(self, copies, buf, base):
        for peer, me, device, number in copies:
            pltpu.make_async_remote_copy(
                src_ref=buf.at[me], dst_ref=buf.at[me], send_sem=self.send.at[number],
                recv_sem=self.recv.at[base + me], device_id=device, device_id_type=MESH,
            ).start()

    def collect(self, copies, buf, base):
        for peer, _, device, number in copies:
            pltpu.make_async_remote_copy(
                src_ref=buf.at[peer], dst_ref=buf.at[peer], send_sem=self.send.at[number],
                recv_sem=self.recv.at[base + peer], device_id=device, device_id_type=MESH,
            ).wait_recv()

    def drain(self, copies, buf, base):
        for peer, me, device, number in copies:
            pltpu.make_async_remote_copy(
                src_ref=buf.at[me], dst_ref=buf.at[me], send_sem=self.send.at[number],
                recv_sem=self.recv.at[base + me], device_id=device, device_id_type=MESH,
            ).wait_send()

    def first(self):
        return self.pair_copy(self.loc.at[1 - self.core], self.inp, 0)

    def last(self):
        return self.pair_copy(self.out.at[self.core], self.out.at[self.core], 1)

    def start_pair(self):
        self.first().start()

    def start_plane(self):
        self.first().wait_recv()
        self.plane[self.iyc * self.nz + self.iz] = self.loc[self.core] + self.inp[...]
        self.spread(self.plane_copies(), self.plane, 2)

    def start_line(self):
        self.collect(self.plane_copies(), self.plane, 2)
        self.line[self.iy] = total_of(self.plane)
        self.spread(self.line_copies(), self.line, 2 + (self.nx // 2) * self.nz)

    def start_share(self):
        self.collect(self.line_copies(), self.line, 2 + (self.nx // 2) * self.nz)
        self.out[self.core] = total_of(self.line)
        self.last().start()

    def result(self):
        other = self.out.at[1 - self.core]
        self.pair_copy(other, other, 1).wait_recv()
        return self.out[0], self.out[1]

    def finish(self):
        self.first().wait_send()
        self.drain(self.plane_copies(), self.plane, 2)
        self.drain(self.line_copies(), self.line, 2 + (self.nx // 2) * self.nz)


def total_of(ref):
    parts = [ref[place] for place in range(ref.shape[0])]
    while len(parts) > 1:
        parts = [sum(parts[k:k + 2][1:], parts[k]) for k in range(0, len(parts), 2)]
    return parts[0]


def fold_history(pairs):
    rows = jnp.concatenate(thirds(keep_same_row(pairs)), axis=0)
    pick = ((iota((8 * HIST, 128), 0) // 8) == iota((8 * HIST, 128), 1)).astype(BF16)
    parts = bdot(rows, pick, NN)
    full = parts[0:HIST] + parts[HIST:2 * HIST] + parts[2 * HIST:3 * HIST]
    lane = iota((8, 128), 1)
    tiles = []
    for half in range(2):
        low = 8 * half
        tile = jnp.where(lane < 56, full[low:low + 8], 0.0)
        tile = jnp.where((lane >= 56) & (lane < 96), pltpu.roll(full[16 + low:24 + low], 40, 1), tile)
        tile = jnp.where((lane >= 96) & (lane < 120), pltpu.roll(full[32 + low:40 + low], 64, 1), tile)
        if half == 0:
            tile = jnp.where(lane >= 120, pltpu.roll(full[48:56], 72, 1), tile)
        tiles.append(tile)
    return tiles


def unfold_history(tiles):
    lane = iota((8, 128), 1)
    rows = []
    for first, turn in ((0, 0), (16, 88), (32, 64), (48, 56)):
        for tile in tiles[:1] if first == 48 else tiles:
            turned = tile if turn == 0 else pltpu.roll(tile, turn, 1)
            rows.append(jnp.where((lane >= first) & (lane < HIST), turned, 0.0))
    upper = jnp.concatenate(rows, axis=0)
    right = jnp.where(iota((HIST, 128), 1) >= 16 * (iota((HIST, 128), 0) // 16) + 16, upper, 0.0)
    return upper, right


def fold_basis(pairs):
    rows = keep_same_row(pairs)
    rows = jnp.concatenate([rows, jnp.zeros((128 - HIST - COLS, 8 * COLS), F32)], axis=0)
    rows = jnp.concatenate(thirds(rows), axis=0)
    pick = (iota((24, 8 * COLS), 0) == (iota((24, 8 * COLS), 1) // 8)).astype(BF16)
    parts = bdot(pick, rows, NT)
    full = parts[:, 0:128] + parts[:, 128:256] + parts[:, 256:384]
    lane = iota((8, 128), 1)
    one = jnp.where(lane < HIST, full[0:8], jnp.where(lane >= 64, pltpu.roll(full[8:16], 64, 1), 0.0))
    two = jnp.where(lane < HIST, full[16:24], 0.0)
    for part in range(3):
        first = 64 + 20 * part
        turned = pltpu.roll(full[8 * part:8 * part + 8], first - HIST, 1)
        two = jnp.where((lane >= first) & (lane < first + COLS), turned, two)
    return one, two


def unfold_basis(one, two):
    lane = iota((24, 128), 1)
    coef = jnp.concatenate([one, pltpu.roll(one, 64, 1), two], axis=0)
    own = jnp.concatenate([pltpu.roll(two, 128 - 64 - 20 * part, 1) for part in range(3)], axis=0)
    return jnp.where(lane < HIST, coef, 0.0), jnp.where(lane < COLS, own, 0.0)


def cycle_kernel(
    nx, ny, nz,
    hist_hbm, start_hbm, diag_hbm,
    kept, sums,
    xcat, hbuf, main, side, edge, corner, x_send, x_recv, x_own, e_recv, k_recv, weight_main, weight_side,
    g_loc, g_inp, g_plane, g_line, g_out,
    c_loc, c_inp, c_plane, c_line, c_out,
    load_sem, heard, hs_sem, hr_sem, g_send, g_recv, c_send, c_recv,
):
    sizes = (nx, ny, nz)
    gsum = Total(sizes, g_loc, g_inp, g_plane, g_line, g_out, g_send, g_recv)
    csum = Total(sizes, c_loc, c_inp, c_plane, c_line, c_out, c_send, c_recv)
    ix, iy, iz = lax.axis_index("gx"), lax.axis_index("gy"), lax.axis_index("gz")
    load_w = pltpu.make_async_copy(start_hbm, main.at[pl.ds(1, NRHS), pl.ds(4, 8)], load_sem.at[0])
    load_d = pltpu.make_async_copy(diag_hbm, main.at[0, pl.ds(4, 8)], load_sem.at[1])
    load_h = pltpu.make_async_copy(hist_hbm, hbuf, load_sem.at[2])
    load_w.start()
    load_d.start()
    load_h.start()

    barrier = pltpu.get_barrier_semaphore()
    nyc, core = nx // 2, lax.rem(ix, 2)
    reach = max(1, ny // 8)

    def far_off(dy, dz):
        return {"gx": 2 * lax.rem(ix // 2 + dy, nyc) + core, "gz": lax.rem(iz + dz, nz)}

    def hops(step, count):
        return min(step, count - step)

    greeted = [{"gx": lax.rem(ix + 1, nx)}, {"gx": lax.rem(ix + nx - 1, nx)}]
    for dy in range(nyc):
        for dz in range(nz):
            if 1 <= hops(dy, nyc) + hops(dz, nz) <= 2:
                greeted.append(far_off(dy, dz))
    for step in range(1, reach + 1):
        greeted += [{"gy": lax.rem(iy + step, ny)}, {"gy": lax.rem(iy + ny - step, ny)}]
    for dy in (1, ny - 1):
        for dz in (1, nz - 1):
            greeted.append({"gy": lax.rem(iy + dy, ny), "gz": lax.rem(iz + dz, nz)})

    def tell(number, device):
        pl.semaphore_signal(heard.at[number], inc=1, device_id=device, device_id_type=MESH)

    def tell_line(number, step):
        tell(number, {"gy": lax.rem(iy + step, ny)})
        tell(number + 1, {"gy": lax.rem(iy + ny - step, ny)})

    def hear(*numbers):
        for number in numbers:
            pl.semaphore_wait(heard.at[number], 1)

    low_x, high_x = ix == 0, ix == nx - 1
    low_y, high_y = iy == 0, iy == ny - 1
    low_z, high_z = iz == 0, iz == nz - 1
    places = 1 + NRHS
    zero = jnp.zeros((places, 8, 128), F32)
    half = jnp.zeros((places, 4, 128), F32)
    side[0:places, 0] = zero
    side[0:places, 15] = zero
    for at, outside in ((0, low_x), (1, high_x)):
        @pl.when(outside)
        def _():
            x_recv[at] = zero
    for at, outside in ((0, low_y), (1, high_y)):
        rows = pl.ds(4 - 4 * at, 4)

        @pl.when(outside)
        def _():
            for z in range(1, 15):
                side[0:places, z, rows] = half
            for third in range(3):
                k_recv[third, :, rows] = half
    for at, outside in ((0, low_z), (1, high_z)):
        @pl.when(outside)
        def _():
            e_recv[at] = zero
            k_recv[1 + at] = zero
            for z in range(12 * at, 12 * at + 4):
                main[0:places, z] = zero
                side[0:places, z] = zero

    for device in greeted:
        pl.semaphore_signal(barrier, inc=1, device_id=device, device_id_type=MESH)

    lane = iota((8, 128), 1)
    row = iota((8, 128), 0)

    def there(dx, dy, dz):
        out = jnp.bool_(True)
        for step, me, count in ((dx, ix, nx), (dy, iy, ny), (dz, iz, nz)):
            if step:
                out = jnp.logical_and(out, me + step >= 0 if step < 0 else me + step < count)
        return out

    def message(number, dx, dy, dz, src, dst):
        device = {}
        for axis, step, me, count in (("gx", dx, ix, nx), ("gy", dy, iy, ny), ("gz", dz, iz, nz)):
            if step:
                device[axis] = lax.rem(me + step + count, count)
        copy = pltpu.make_async_remote_copy(
            src_ref=src, dst_ref=dst, send_sem=hs_sem.at[number], recv_sem=hr_sem.at[number],
            device_id=device, device_id_type=MESH,
        )
        return there(dx, dy, dz), there(-dx, -dy, -dz), copy

    few = pl.ds(0, places)
    rows_of = {1: pl.ds(4, 4), -1: pl.ds(0, 4)}
    first = [message(0, 1, 0, 0, x_send, x_recv.at[0]), message(1, -1, 0, 0, x_send, x_recv.at[1])]
    first.append(message(2, 0, 0, 1, main.at[few, pl.ds(8, 4)], main.at[few, pl.ds(0, 4)]))
    first.append(message(3, 0, 0, -1, main.at[few, pl.ds(4, 4)], main.at[few, pl.ds(12, 4)]))
    second = [message(4, 0, 0, 1, x_own, e_recv.at[0]), message(5, 0, 0, -1, x_own, e_recv.at[1])]
    for k, dy in enumerate((1, -1)):
        rows = rows_of[dy]
        first.append(message(
            6 + k, 0, dy, 0, main.at[few, pl.ds(4, 8), rows], side.at[few, pl.ds(4, 8), rows]))
        second.append(message(8 + k, 0, dy, 0, x_own.at[:, rows], k_recv.at[0, :, rows]))
        for n, dz in enumerate((1, -1)):
            src = pl.ds(9 if dz > 0 else 4, 3)
            dst = pl.ds(1 if dz > 0 else 12, 3)
            first.append(message(
                10 + 2 * k + n, 0, dy, dz, main.at[few, src, rows], side.at[few, dst, rows]))
            second.append(message(14 + 2 * k + n, 0, dy, dz, x_own.at[:, rows], k_recv.at[1 + n, :, rows]))

    def send(messages):
        for sends, _, copy in messages:
            @pl.when(sends)
            def _():
                copy.start()

    def receive(messages):
        for _, comes, copy in messages:
            @pl.when(comes)
            def _():
                copy.wait_recv()

    def leave(messages):
        for sends, _, copy in messages:
            @pl.when(sends)
            def _():
                copy.wait_send()

    def keep_split(level):
        for z in range(8):
            block = main[1 + NRHS * level:1 + NRHS * (level + 1), 4 + z].reshape(8 * NRHS, 128)
            top, low = split(block)
            rows = pl.ds(8 * (HIST + NRHS * level), 8 * NRHS)
            xcat[rows, 128 * z:128 * (z + 1)] = top
            xcat[rows, 1024 + 128 * z:1024 + 128 * (z + 1)] = low

    def turn(value, by, axis):
        by = by % value.shape[axis]
        return value if by == 0 else pltpu.roll(value, by, axis)

    inside = lambda outside: jnp.where(outside, 0.0, 1.0).astype(F32)
    in_z = [inside(low_z) if z < 4 else (inside(high_z) if z > 11 else 1.0) for z in range(16)]
    in_y = jnp.where(row < 4, inside(high_y), inside(low_y))
    in_x = jnp.where(lane % 8 < 4, inside(high_x), inside(low_x))
    in_x = in_x * jnp.where((lane >= 28) & (lane < 92), 1.0, jnp.where((lane >= 92) & (lane < 124), in_z[12], in_z[0]))
    seventh = 1.0 / 7.0

    def beside_x(value, turned):
        at = iota(value.shape, 2)
        left = turn(jnp.where(at == 127, turned, value), 1, 2)
        return left + turn(jnp.where(at == 0, turned, value), -1, 2)

    def beside_y(inner, outer):
        at = iota(inner.shape, inner.ndim - 2)
        inner_low, outer_low = turn(inner, 1, inner.ndim - 2), turn(outer, 1, inner.ndim - 2)
        inner_high, outer_high = turn(inner, -1, inner.ndim - 2), turn(outer, -1, inner.ndim - 2)
        return (
            jnp.where(at == 0, outer_low, inner_low) + jnp.where(at == 7, outer_high, inner_high),
            jnp.where(at == 0, inner_low, outer_low) + jnp.where(at == 7, inner_high, outer_high),
        )

    def beside_edge(value, ends):
        left = jnp.where(lane % 8 == 0, turn(ends, 1, 1), turn(value, 1, 1))
        right = jnp.where(lane % 8 == 7, turn(ends, -1, 1), turn(value, -1, 1))
        return left + right + turn(value, 8, 1) + turn(value, -8, 1)

    def spread(value, low, high):
        return jnp.concatenate([turn(value, -8 * z, 1)[None] for z in range(low, high)], axis=0)

    def ends_of(base, value, low, high):
        turned = [turn(value[z - low], 8 * z, 1) for z in range(low, high)]
        for z in range(low, high):
            base = jnp.where((lane == 8 * z) | (lane == (8 * z + 127) % 128), turned[z - low], base)
        return base

    def advance(level):
        more = level < STEPS - 1
        low, high = level + 1, 15 - level

        def vector(f, carry):
            at = 1 + NRHS * level + f

            def follow(scaled, ref, *place):
                if level > 0:
                    scaled = 2.0 * scaled - ref[(at - NRHS, *place)]
                ref[(at + NRHS, *place)] = scaled

            v, u = main[at, low:high], side[at, low:high]
            edge_v, corner_v = edge[at], corner[at]
            turned = spread(edge_v, low, high)
            if more:
                turned_u = spread(corner_v, low + 1, high - 1)
                ends = ends_of(edge_v, v, low, high)
                side_ends = ends_of(corner_v, u, low, high)
            across = beside_x(v, turned)
            if more:
                across_u = beside_x(u[1:-1], turned_u)
            near, far = beside_y(v, u)
            near = near + across + main[at, low - 1:high - 1] + main[at, low + 1:high + 1]
            follow(main[0, low:high] * v - near * weight_main[low:high], main, slice(low, high))
            if more:
                far = far[1:-1] + across_u + side[at, low:high - 2] + side[at, low + 2:high]
                follow(
                    side[0, low + 1:high - 1] * u[1:-1] - far * weight_side[low + 1:high - 1],
                    side, slice(low + 1, high - 1),
                )
                near, far = beside_y(edge_v, corner_v)
                near = near + beside_edge(edge_v, ends)
                far = far + beside_edge(corner_v, side_ends)
                follow(edge[0] * edge_v - near * (in_x * seventh), edge)
                follow(corner[0] * corner_v - far * (in_x * in_y * seventh), corner)
            return carry

        lax.fori_loop(0, NRHS, vector, 0)

    load_w.wait()
    load_d.wait()
    for place in range(places):
        packed = jnp.zeros((8, 128), F32)
        for z in range(4, 12):
            here = (lane >= 8 * z - 4) & (lane < 8 * z + 4)
            packed = jnp.where(here, turn(main[place, z], 8 * z, 1), packed)
        x_send[place] = packed
    pl.semaphore_wait(barrier, len(greeted))
    send(first)
    if nyc > 1:
        tell(0, far_off(nyc // 2, 0))
    if nz > 1:
        tell(1, far_off(0, nz // 2))
    tell_line(2, reach)

    load_h.wait()
    for z in range(8):
        top, low = split(hbuf[:, z].reshape(8 * HIST, 128))
        xcat[0:8 * HIST, 128 * z:128 * (z + 1)] = top
        xcat[0:8 * HIST, 1024 + 128 * z:1024 + 128 * (z + 1)] = low
    receive(first[:2])
    for place in range(places):
        x_own[place] = jnp.where(lane % 8 >= 4, x_recv[0, place], x_recv[1, place])
    send(second)
    hear(2, 3)
    tell_line(4, 2 * reach)
    top, low = xcat[0:8 * HIST, 0:1024], xcat[0:8 * HIST, 1024:2048]
    pairs = bdot(top, top, NT) + bdot(top, low, NT) + bdot(low, top, NT)
    g_loc[0], g_loc[1] = fold_history(pairs)
    gsum.start_pair()
    keep_split(0)

    receive(first[2:])
    receive(second)
    leave(first)
    hear(*([0] if nyc > 1 else []), *([1] if nz > 1 else []))
    gsum.start_plane()
    own = (lane >= 28) & (lane < 92)
    for place in range(places):
        above = turn(jnp.where(lane < 60, e_recv[1, place], e_recv[0, place]), 64, 1)
        edge[place] = jnp.where(own, x_own[place], above)
        above = turn(jnp.where(lane < 60, k_recv[2, place], k_recv[1, place]), 64, 1)
        corner[place] = jnp.where(own, k_recv[0, place], above)
    for z in range(1, 15):
        scaled = (main[0, z] - 1.0) * seventh
        main[0, z] = scaled if 4 <= z < 12 else scaled * in_z[z]
        scaled = (side[0, z] - 1.0) * (in_y * seventh)
        side[0, z] = scaled if 4 <= z < 12 else scaled * in_z[z]
    edge[0] = (edge[0] - 1.0) * (in_x * seventh)
    corner[0] = (corner[0] - 1.0) * (in_x * in_y * seventh)
    for z in range(16):
        weight_main[z] = jnp.full((8, 128), seventh * in_z[z], F32)
        weight_side[z] = in_y * (seventh * in_z[z])
    for level in range(STEPS):
        advance(level)
        keep_split(level + 1)
    store = pltpu.make_async_copy(xcat, kept, load_sem.at[0])
    store.start()

    wt = xcat[8 * HIST:8 * (HIST + COLS), 0:1024]
    wl = xcat[8 * HIST:8 * (HIST + COLS), 1024:2048]
    xt, xl = xcat[:, 0:1024], xcat[:, 1024:2048]
    pairs = bdot(xt, wt, NT) + bdot(xt, wl, NT) + bdot(xl, wt, NT)
    c_loc[0], c_loc[1] = fold_basis(pairs)
    csum.start_pair()
    hear(4, 5)
    gsum.start_line()
    csum.start_plane()
    leave(second)
    csum.start_line()
    gsum.start_share()
    store.wait()
    sums[2], sums[3] = gsum.result()
    gsum.finish()
    gsum.last().wait_send()
    csum.start_share()
    csum.finish()
    sums[0], sums[1] = csum.result()
    csum.last().wait_send()


def finish_kernel(cells, kept, sums, new_basis, r_out, xcat, done, r_factor, load_sem, store_sem):
    load = pltpu.make_async_copy(kept, xcat, load_sem.at[0])
    load.start()
    scale = 1.0 / cells
    one, two, three, four = [sums[k] * scale for k in range(4)]
    gram_h, right_h = unfold_history([three, four])
    lane = iota((24, 128), 1)
    row = iota((24, 128), 0)
    coef, own = unfold_basis(one, two)
    work = fdot(coef[:, 0:HIST], gram_h, NN) + fdot(coef, jnp.concatenate([right_h, jnp.zeros((72, 128), F32)], axis=0), NT)
    wide = jnp.concatenate([coef, jnp.zeros((104, 128), F32)], axis=0)
    gram = fdot(work - 2.0 * coef, wide, NT) + own
    rhs = jnp.where(lane < HIST, -coef, jnp.where(lane - HIST == row, 1.0, 0.0))

    columns = [jnp.broadcast_to(gram[:, k:k + 1], (24, 128)) for k in range(COLS)]
    lower = jnp.zeros((24, 128), F32)
    for j in range(COLS):
        pivot = jnp.broadcast_to(columns[j][j:j + 1], (24, 128))
        inverse = lax.rsqrt(pivot)
        inverse = inverse * (1.5 - 0.5 * pivot * inverse * inverse)
        column = jnp.where(row >= j, columns[j] * inverse, 0.0)
        lower = jnp.where(lane == j, column, lower)
        solved = jnp.broadcast_to(rhs[j:j + 1], (24, 128)) * inverse
        rhs = jnp.where(row == j, solved, rhs - jnp.where(row > j, column * solved, 0.0))
        for k in range(j + 1, COLS):
            columns[k] = columns[k] - column * jnp.broadcast_to(column[k:k + 1], (24, 128))
    square = jnp.concatenate([lower, jnp.zeros((104, 128), F32)], axis=0)
    r_factor[...] = square.T[0:COLS, 0:COLS]
    store_r = pltpu.make_async_copy(r_factor, r_out, store_sem.at[4])
    store_r.start()

    weights = rhs[0:COLS]
    top, low = split(weights)
    spread = ((iota((128, 8 * (HIST + COLS)), 1) // 8) == iota((128, 8 * (HIST + COLS)), 0)).astype(BF16)
    size = (8 * COLS, 8 * (HIST + COLS))
    same = (iota(size, 0) % 8) == (iota(size, 1) % 8)

    def widen(part):
        wide = bdot(part, spread, NN)
        wide = jnp.broadcast_to(wide[:, None, :], (COLS, 8, size[1])).reshape(size)
        return jnp.where(same, wide, 0.0).astype(BF16)

    top, low = widen(top), widen(low)
    load.wait()
    stores = []
    for part in range(4):
        cols = slice(256 * part, 256 * (part + 1))
        lows = slice(1024 + 256 * part, 1024 + 256 * (part + 1))
        out = bdot(top, xcat[:, cols], NN) + bdot(top, xcat[:, lows], NN) + bdot(low, xcat[:, cols], NN)
        for half in range(2):
            done[:, 2 * part + half] = out[:, 128 * half:128 * (half + 1)].reshape(COLS, 8, 128)
        layers = pl.ds(2 * part, 2)
        stores.append(pltpu.make_async_copy(done.at[:, layers], new_basis.at[:, layers], store_sem.at[part]))
        stores[-1].start()
    for copy in stores:
        copy.wait()
    store_r.wait()


def on_device(nx, ny, nz, history, start, diagonal):
    dma = pltpu.SemaphoreType.DMA
    tiles = lambda *shape: pltpu.VMEM((*shape, 8, 128), F32)
    plane = (nx // 2) * nz
    reduction = [tiles(2), tiles(), tiles(plane), tiles(ny), tiles(2)]
    any_spec = pl.BlockSpec(memory_space=pl.ANY)
    vmem = pl.BlockSpec(memory_space=pltpu.VMEM)
    cells = float(nx * ny * nz * diagonal.size)
    kept, sums = pl.pallas_call(
        functools.partial(cycle_kernel, nx, ny, nz),
        name="cycle",
        out_shape=(
            jax.ShapeDtypeStruct((8 * (HIST + COLS), 2048), BF16),
            jax.ShapeDtypeStruct((4, 8, 128), F32),
        ),
        in_specs=[any_spec] * 3,
        out_specs=(any_spec, vmem),
        scratch_shapes=[
            pltpu.VMEM((8 * (HIST + COLS), 2048), BF16),
            tiles(HIST, 8),
            tiles(1 + COLS, 16),
            tiles(1 + NRHS * STEPS, 16),
            tiles(1 + NRHS * STEPS),
            tiles(1 + NRHS * STEPS),
            tiles(1 + NRHS),
            tiles(2, 1 + NRHS),
            tiles(1 + NRHS),
            tiles(2, 1 + NRHS),
            tiles(3, 1 + NRHS),
            tiles(16),
            tiles(16),
            *reduction,
            *reduction,
            dma((3,)), pltpu.SemaphoreType.REGULAR((6,)), dma((18,)), dma((18,)),
            *[dma((2 + plane + ny,))] * 4,
        ],
        compiler_params=pltpu.CompilerParams(
            collective_id=0, has_side_effects=True, vmem_limit_bytes=VMEM_BYTES
        ),
    )(history, start, diagonal)
    return pl.pallas_call(
        functools.partial(finish_kernel, cells),
        name="finish",
        out_shape=(
            jax.ShapeDtypeStruct((COLS, 8, 8, 128), F32),
            jax.ShapeDtypeStruct((COLS, COLS), F32),
        ),
        in_specs=[any_spec, vmem],
        out_specs=(any_spec, any_spec),
        scratch_shapes=[
            pltpu.VMEM((8 * (HIST + COLS), 2048), BF16),
            tiles(COLS, 8),
            pltpu.VMEM((COLS, COLS), F32),
            dma((1,)),
            dma((5,)),
        ],
        compiler_params=pltpu.CompilerParams(vmem_limit_bytes=VMEM_BYTES),
    )(kept, sums)


def solution(mesh):
    return jax.shard_map(
        functools.partial(on_device, mesh.shape["gx"], mesh.shape["gy"], mesh.shape["gz"]),
        mesh=mesh,
        in_specs=(P(None, "gz", "gy", "gx"), P(None, "gz", "gy", "gx"), P("gz", "gy", "gx")),
        out_specs=(P(None, "gz", "gy", "gx"), P()),
        check_vma=False,
    )
```

```python
import functools

import jax
import jax.numpy as jnp
from jax import lax
from jax.experimental import pallas as pl
from jax.experimental.pallas import tpu as pltpu
from jax.sharding import PartitionSpec as P

STEPS = 4
NRHS = 4
HIST = 56
COLS = 20
MESH = pl.DeviceIdType.MESH
F32 = jnp.float32
BF16 = jnp.bfloat16
NT = (((1,), (1,)), ((), ()))
NN = (((1,), (0,)), ((), ()))
HIGH = lax.Precision.HIGHEST
VMEM_BYTES = 56_520_000


def iota(shape, dim):
    return lax.broadcasted_iota(jnp.int32, shape, dim)


def split(value):
    top = value.astype(BF16)
    return top, (value - top.astype(F32)).astype(BF16)


def bdot(left, right, dims):
    return lax.dot_general(left, right, dims, preferred_element_type=F32)


def fdot(left, right, dims):
    return lax.dot_general(left, right, dims, precision=HIGH, preferred_element_type=F32)


def keep_same_row(value):
    same = (iota(value.shape, 0) % 8) == (iota(value.shape, 1) % 8)
    masked = jnp.where(same, value, 0.0)
    return jnp.sum(masked.reshape(value.shape[0] // 8, 8, value.shape[1]), axis=1)


def thirds(value):
    first = value.astype(BF16)
    rest = value - first.astype(F32)
    second = rest.astype(BF16)
    return first, second, (rest - second.astype(F32)).astype(BF16)


class Total:
    def __init__(self, sizes, loc, inp, plane, line, out, send, recv):
        self.nx, self.ny, self.nz = sizes
        self.loc, self.inp, self.plane, self.line, self.out = loc, inp, plane, line, out
        self.send, self.recv = send, recv
        self.ix, self.iy, self.iz = lax.axis_index("gx"), lax.axis_index("gy"), lax.axis_index("gz")
        self.core = lax.rem(self.ix, 2)
        self.iyc = self.ix // 2

    def pair_copy(self, src, dst, number):
        return pltpu.make_async_remote_copy(
            src_ref=src, dst_ref=dst, send_sem=self.send.at[number], recv_sem=self.recv.at[number],
            device_id={"gx": self.ix + 1 - 2 * self.core}, device_id_type=MESH,
        )

    def plane_copies(self):
        nyc, nz = self.nx // 2, self.nz
        for step in range(1, nyc * nz):
            py = lax.rem(self.iyc + step // nz, nyc)
            pz = lax.rem(self.iz + step % nz, nz)
            yield py * nz + pz, self.iyc * nz + self.iz, {"gx": 2 * py + self.core, "gz": pz}, 2 + step

    def line_copies(self):
        for step in range(1, self.ny):
            peer = lax.rem(self.iy + step, self.ny)
            yield peer, self.iy, {"gy": peer}, 2 + (self.nx // 2) * self.nz + step

    def spread(self, copies, buf, base):
        for peer, me, device, number in copies:
            pltpu.make_async_remote_copy(
                src_ref=buf.at[me], dst_ref=buf.at[me], send_sem=self.send.at[number],
                recv_sem=self.recv.at[base + me], device_id=device, device_id_type=MESH,
            ).start()

    def collect(self, copies, buf, base):
        for peer, _, device, number in copies:
            pltpu.make_async_remote_copy(
                src_ref=buf.at[peer], dst_ref=buf.at[peer], send_sem=self.send.at[number],
                recv_sem=self.recv.at[base + peer], device_id=device, device_id_type=MESH,
            ).wait_recv()

    def drain(self, copies, buf, base):
        for peer, me, device, number in copies:
            pltpu.make_async_remote_copy(
                src_ref=buf.at[me], dst_ref=buf.at[me], send_sem=self.send.at[number],
                recv_sem=self.recv.at[base + me], device_id=device, device_id_type=MESH,
            ).wait_send()

    def first(self):
        return self.pair_copy(self.loc.at[1 - self.core], self.inp, 0)

    def last(self):
        return self.pair_copy(self.out.at[self.core], self.out.at[self.core], 1)

    def start_pair(self):
        self.first().start()

    def start_plane(self):
        self.first().wait_recv()
        self.plane[self.iyc * self.nz + self.iz] = self.loc[self.core] + self.inp[...]
        self.spread(self.plane_copies(), self.plane, 2)

    def start_line(self):
        self.collect(self.plane_copies(), self.plane, 2)
        self.line[self.iy] = total_of(self.plane)
        self.spread(self.line_copies(), self.line, 2 + (self.nx // 2) * self.nz)

    def start_share(self):
        self.collect(self.line_copies(), self.line, 2 + (self.nx // 2) * self.nz)
        self.out[self.core] = total_of(self.line)
        self.last().start()

    def result(self):
        other = self.out.at[1 - self.core]
        self.pair_copy(other, other, 1).wait_recv()
        return self.out[0], self.out[1]

    def finish(self):
        self.first().wait_send()
        self.drain(self.plane_copies(), self.plane, 2)
        self.drain(self.line_copies(), self.line, 2 + (self.nx // 2) * self.nz)


def total_of(ref):
    parts = [ref[place] for place in range(ref.shape[0])]
    while len(parts) > 1:
        parts = [sum(parts[k:k + 2][1:], parts[k]) for k in range(0, len(parts), 2)]
    return parts[0]


def fold_history(pairs):
    rows = jnp.concatenate(thirds(keep_same_row(pairs)), axis=0)
    pick = ((iota((8 * HIST, 128), 0) // 8) == iota((8 * HIST, 128), 1)).astype(BF16)
    parts = bdot(rows, pick, NN)
    full = parts[0:HIST] + parts[HIST:2 * HIST] + parts[2 * HIST:3 * HIST]
    lane = iota((8, 128), 1)
    tiles = []
    for half in range(2):
        low = 8 * half
        tile = jnp.where(lane < 56, full[low:low + 8], 0.0)
        tile = jnp.where((lane >= 56) & (lane < 96), pltpu.roll(full[16 + low:24 + low], 40, 1), tile)
        tile = jnp.where((lane >= 96) & (lane < 120), pltpu.roll(full[32 + low:40 + low], 64, 1), tile)
        if half == 0:
            tile = jnp.where(lane >= 120, pltpu.roll(full[48:56], 72, 1), tile)
        tiles.append(tile)
    return tiles


def unfold_history(tiles):
    lane = iota((8, 128), 1)
    rows = []
    for first, turn in ((0, 0), (16, 88), (32, 64), (48, 56)):
        for tile in tiles[:1] if first == 48 else tiles:
            turned = tile if turn == 0 else pltpu.roll(tile, turn, 1)
            rows.append(jnp.where((lane >= first) & (lane < HIST), turned, 0.0))
    upper = jnp.concatenate(rows, axis=0)
    right = jnp.where(iota((HIST, 128), 1) >= 16 * (iota((HIST, 128), 0) // 16) + 16, upper, 0.0)
    return upper, right


def fold_basis(pairs):
    rows = keep_same_row(pairs)
    rows = jnp.concatenate([rows, jnp.zeros((128 - HIST - COLS, 8 * COLS), F32)], axis=0)
    rows = jnp.concatenate(thirds(rows), axis=0)
    pick = (iota((24, 8 * COLS), 0) == (iota((24, 8 * COLS), 1) // 8)).astype(BF16)
    parts = bdot(pick, rows, NT)
    full = parts[:, 0:128] + parts[:, 128:256] + parts[:, 256:384]
    lane = iota((8, 128), 1)
    one = jnp.where(lane < HIST, full[0:8], jnp.where(lane >= 64, pltpu.roll(full[8:16], 64, 1), 0.0))
    two = jnp.where(lane < HIST, full[16:24], 0.0)
    for part in range(3):
        first = 64 + 20 * part
        turned = pltpu.roll(full[8 * part:8 * part + 8], first - HIST, 1)
        two = jnp.where((lane >= first) & (lane < first + COLS), turned, two)
    return one, two


def unfold_basis(one, two):
    lane = iota((24, 128), 1)
    coef = jnp.concatenate([one, pltpu.roll(one, 64, 1), two], axis=0)
    own = jnp.concatenate([pltpu.roll(two, 128 - 64 - 20 * part, 1) for part in range(3)], axis=0)
    return jnp.where(lane < HIST, coef, 0.0), jnp.where(lane < COLS, own, 0.0)


def cycle_kernel(
    nx, ny, nz,
    hist_hbm, start_hbm, diag_hbm,
    kept, sums,
    xcat, hbuf, main, side, edge, corner, x_send, x_recv, x_own, e_recv, k_recv, weight_main, weight_side,
    g_loc, g_inp, g_plane, g_line, g_out,
    c_loc, c_inp, c_plane, c_line, c_out,
    load_sem, heard, hs_sem, hr_sem, g_send, g_recv, c_send, c_recv,
):
    sizes = (nx, ny, nz)
    gsum = Total(sizes, g_loc, g_inp, g_plane, g_line, g_out, g_send, g_recv)
    csum = Total(sizes, c_loc, c_inp, c_plane, c_line, c_out, c_send, c_recv)
    ix, iy, iz = lax.axis_index("gx"), lax.axis_index("gy"), lax.axis_index("gz")
    load_w = pltpu.make_async_copy(start_hbm, main.at[pl.ds(1, NRHS), pl.ds(4, 8)], load_sem.at[0])
    load_d = pltpu.make_async_copy(diag_hbm, main.at[0, pl.ds(4, 8)], load_sem.at[1])
    load_h = pltpu.make_async_copy(hist_hbm, hbuf, load_sem.at[2])
    load_w.start()
    load_d.start()
    load_h.start()

    barrier = pltpu.get_barrier_semaphore()
    nyc, core = nx // 2, lax.rem(ix, 2)
    reach = max(1, ny // 8)

    def far_off(dy, dz):
        return {"gx": 2 * lax.rem(ix // 2 + dy, nyc) + core, "gz": lax.rem(iz + dz, nz)}

    def hops(step, count):
        return min(step, count - step)

    greeted = [{"gx": lax.rem(ix + 1, nx)}, {"gx": lax.rem(ix + nx - 1, nx)}]
    for dy in range(nyc):
        for dz in range(nz):
            if 1 <= hops(dy, nyc) + hops(dz, nz) <= 2:
                greeted.append(far_off(dy, dz))
    for step in range(1, reach + 1):
        greeted += [{"gy": lax.rem(iy + step, ny)}, {"gy": lax.rem(iy + ny - step, ny)}]
    for dy in (1, ny - 1):
        for dz in (1, nz - 1):
            greeted.append({"gy": lax.rem(iy + dy, ny), "gz": lax.rem(iz + dz, nz)})

    def tell(number, device):
        pl.semaphore_signal(heard.at[number], inc=1, device_id=device, device_id_type=MESH)

    def tell_line(number, step):
        tell(number, {"gy": lax.rem(iy + step, ny)})
        tell(number + 1, {"gy": lax.rem(iy + ny - step, ny)})

    def hear(*numbers):
        for number in numbers:
            pl.semaphore_wait(heard.at[number], 1)

    low_x, high_x = ix == 0, ix == nx - 1
    low_y, high_y = iy == 0, iy == ny - 1
    low_z, high_z = iz == 0, iz == nz - 1
    places = 1 + NRHS
    zero = jnp.zeros((places, 8, 128), F32)
    half = jnp.zeros((places, 4, 128), F32)
    side[0:places, 0] = zero
    side[0:places, 15] = zero
    for at, outside in ((0, low_x), (1, high_x)):
        @pl.when(outside)
        def _():
            x_recv[at] = zero
    for at, outside in ((0, low_y), (1, high_y)):
        rows = pl.ds(4 - 4 * at, 4)

        @pl.when(outside)
        def _():
            for z in range(1, 15):
                side[0:places, z, rows] = half
            for third in range(3):
                k_recv[third, :, rows] = half
    for at, outside in ((0, low_z), (1, high_z)):
        @pl.when(outside)
        def _():
            e_recv[at] = zero
            k_recv[1 + at] = zero
            for z in range(12 * at, 12 * at + 4):
                main[0:places, z] = zero
                side[0:places, z] = zero

    for device in greeted:
        pl.semaphore_signal(barrier, inc=1, device_id=device, device_id_type=MESH)

    lane = iota((8, 128), 1)
    row = iota((8, 128), 0)

    def there(dx, dy, dz):
        out = jnp.bool_(True)
        for step, me, count in ((dx, ix, nx), (dy, iy, ny), (dz, iz, nz)):
            if step:
                out = jnp.logical_and(out, me + step >= 0 if step < 0 else me + step < count)
        return out

    def message(number, dx, dy, dz, src, dst):
        device = {}
        for axis, step, me, count in (("gx", dx, ix, nx), ("gy", dy, iy, ny), ("gz", dz, iz, nz)):
            if step:
                device[axis] = lax.rem(me + step + count, count)
        copy = pltpu.make_async_remote_copy(
            src_ref=src, dst_ref=dst, send_sem=hs_sem.at[number], recv_sem=hr_sem.at[number],
            device_id=device, device_id_type=MESH,
        )
        return there(dx, dy, dz), there(-dx, -dy, -dz), copy

    few = pl.ds(0, places)
    rows_of = {1: pl.ds(4, 4), -1: pl.ds(0, 4)}
    first = [message(0, 1, 0, 0, x_send, x_recv.at[0]), message(1, -1, 0, 0, x_send, x_recv.at[1])]
    first.append(message(2, 0, 0, 1, main.at[few, pl.ds(8, 4)], main.at[few, pl.ds(0, 4)]))
    first.append(message(3, 0, 0, -1, main.at[few, pl.ds(4, 4)], main.at[few, pl.ds(12, 4)]))
    second = [message(4, 0, 0, 1, x_own, e_recv.at[0]), message(5, 0, 0, -1, x_own, e_recv.at[1])]
    for k, dy in enumerate((1, -1)):
        rows = rows_of[dy]
        first.append(message(
            6 + k, 0, dy, 0, main.at[few, pl.ds(4, 8), rows], side.at[few, pl.ds(4, 8), rows]))
        second.append(message(8 + k, 0, dy, 0, x_own.at[:, rows], k_recv.at[0, :, rows]))
        for n, dz in enumerate((1, -1)):
            src = pl.ds(9 if dz > 0 else 4, 3)
            dst = pl.ds(1 if dz > 0 else 12, 3)
            first.append(message(
                10 + 2 * k + n, 0, dy, dz, main.at[few, src, rows], side.at[few, dst, rows]))
            second.append(message(14 + 2 * k + n, 0, dy, dz, x_own.at[:, rows], k_recv.at[1 + n, :, rows]))

    def send(messages):
        for sends, _, copy in messages:
            @pl.when(sends)
            def _():
                copy.start()

    def receive(messages):
        for _, comes, copy in messages:
            @pl.when(comes)
            def _():
                copy.wait_recv()

    def leave(messages):
        for sends, _, copy in messages:
            @pl.when(sends)
            def _():
                copy.wait_send()

    def keep_split(level):
        for z in range(8):
            block = main[1 + NRHS * level:1 + NRHS * (level + 1), 4 + z].reshape(8 * NRHS, 128)
            top, low = split(block)
            rows = pl.ds(8 * (HIST + NRHS * level), 8 * NRHS)
            xcat[rows, 128 * z:128 * (z + 1)] = top
            xcat[rows, 1024 + 128 * z:1024 + 128 * (z + 1)] = low

    def turn(value, by, axis):
        by = by % value.shape[axis]
        return value if by == 0 else pltpu.roll(value, by, axis)

    inside = lambda outside: jnp.where(outside, 0.0, 1.0).astype(F32)
    in_z = [inside(low_z) if z < 4 else (inside(high_z) if z > 11 else 1.0) for z in range(16)]
    in_y = jnp.where(row < 4, inside(high_y), inside(low_y))
    in_x = jnp.where(lane % 8 < 4, inside(high_x), inside(low_x))
    in_x = in_x * jnp.where((lane >= 28) & (lane < 92), 1.0, jnp.where((lane >= 92) & (lane < 124), in_z[12], in_z[0]))
    seventh = 1.0 / 7.0

    def beside_x(value, turned):
        at = iota(value.shape, 2)
        left = turn(jnp.where(at == 127, turned, value), 1, 2)
        return left + turn(jnp.where(at == 0, turned, value), -1, 2)

    def beside_y(inner, outer):
        at = iota(inner.shape, inner.ndim - 2)
        inner_low, outer_low = turn(inner, 1, inner.ndim - 2), turn(outer, 1, inner.ndim - 2)
        inner_high, outer_high = turn(inner, -1, inner.ndim - 2), turn(outer, -1, inner.ndim - 2)
        return (
            jnp.where(at == 0, outer_low, inner_low) + jnp.where(at == 7, outer_high, inner_high),
            jnp.where(at == 0, inner_low, outer_low) + jnp.where(at == 7, inner_high, outer_high),
        )

    def beside_edge(value, ends):
        left = jnp.where(lane % 8 == 0, turn(ends, 1, 1), turn(value, 1, 1))
        right = jnp.where(lane % 8 == 7, turn(ends, -1, 1), turn(value, -1, 1))
        return left + right + turn(value, 8, 1) + turn(value, -8, 1)

    def spread(value, low, high):
        return jnp.concatenate([turn(value, -8 * z, 1)[None] for z in range(low, high)], axis=0)

    def ends_of(base, value, low, high):
        turned = [turn(value[z - low], 8 * z, 1) for z in range(low, high)]
        for z in range(low, high):
            base = jnp.where((lane == 8 * z) | (lane == (8 * z + 127) % 128), turned[z - low], base)
        return base

    def advance(level):
        more = level < STEPS - 1
        low, high = level + 1, 15 - level

        def vector(f, carry):
            at = 1 + NRHS * level + f

            def follow(scaled, ref, *place):
                if level > 0:
                    scaled = 2.0 * scaled - ref[(at - NRHS, *place)]
                ref[(at + NRHS, *place)] = scaled

            v, u = main[at, low:high], side[at, low:high]
            edge_v, corner_v = edge[at], corner[at]
            turned = spread(edge_v, low, high)
            if more:
                turned_u = spread(corner_v, low + 1, high - 1)
                ends = ends_of(edge_v, v, low, high)
                side_ends = ends_of(corner_v, u, low, high)
            across = beside_x(v, turned)
            if more:
                across_u = beside_x(u[1:-1], turned_u)
            near, far = beside_y(v, u)
            near = near + across + main[at, low - 1:high - 1] + main[at, low + 1:high + 1]
            follow(main[0, low:high] * v - near * weight_main[low:high], main, slice(low, high))
            if more:
                far = far[1:-1] + across_u + side[at, low:high - 2] + side[at, low + 2:high]
                follow(
                    side[0, low + 1:high - 1] * u[1:-1] - far * weight_side[low + 1:high - 1],
                    side, slice(low + 1, high - 1),
                )
                near, far = beside_y(edge_v, corner_v)
                near = near + beside_edge(edge_v, ends)
                far = far + beside_edge(corner_v, side_ends)
                follow(edge[0] * edge_v - near * (in_x * seventh), edge)
                follow(corner[0] * corner_v - far * (in_x * in_y * seventh), corner)
            return carry

        lax.fori_loop(0, NRHS, vector, 0, unroll=4)

    load_w.wait()
    load_d.wait()
    for place in range(places):
        packed = jnp.zeros((8, 128), F32)
        for z in range(4, 12):
            here = (lane >= 8 * z - 4) & (lane < 8 * z + 4)
            packed = jnp.where(here, turn(main[place, z], 8 * z, 1), packed)
        x_send[place] = packed
    pl.semaphore_wait(barrier, len(greeted))
    send(first)
    if nyc > 1:
        tell(0, far_off(nyc // 2, 0))
    if nz > 1:
        tell(1, far_off(0, nz // 2))
    tell_line(2, reach)

    load_h.wait()
    for z in range(8):
        top, low = split(hbuf[:, z].reshape(8 * HIST, 128))
        xcat[0:8 * HIST, 128 * z:128 * (z + 1)] = top
        xcat[0:8 * HIST, 1024 + 128 * z:1024 + 128 * (z + 1)] = low
    receive(first[:2])
    for place in range(places):
        x_own[place] = jnp.where(lane % 8 >= 4, x_recv[0, place], x_recv[1, place])
    send(second)
    hear(2, 3)
    tell_line(4, 2 * reach)
    top, low = xcat[0:8 * HIST, 0:1024], xcat[0:8 * HIST, 1024:2048]
    pairs = bdot(top, top, NT) + bdot(top, low, NT) + bdot(low, top, NT) + bdot(low, low, NT)
    g_loc[0], g_loc[1] = fold_history(pairs)
    gsum.start_pair()
    keep_split(0)

    receive(first[2:])
    receive(second)
    leave(first)
    hear(*([0] if nyc > 1 else []), *([1] if nz > 1 else []))
    gsum.start_plane()
    own = (lane >= 28) & (lane < 92)
    for place in range(places):
        above = turn(jnp.where(lane < 60, e_recv[1, place], e_recv[0, place]), 64, 1)
        edge[place] = jnp.where(own, x_own[place], above)
        above = turn(jnp.where(lane < 60, k_recv[2, place], k_recv[1, place]), 64, 1)
        corner[place] = jnp.where(own, k_recv[0, place], above)
    for z in range(1, 15):
        scaled = (main[0, z] - 1.0) * seventh
        main[0, z] = scaled if 4 <= z < 12 else scaled * in_z[z]
        scaled = (side[0, z] - 1.0) * (in_y * seventh)
        side[0, z] = scaled if 4 <= z < 12 else scaled * in_z[z]
    edge[0] = (edge[0] - 1.0) * (in_x * seventh)
    corner[0] = (corner[0] - 1.0) * (in_x * in_y * seventh)
    for z in range(16):
        weight_main[z] = jnp.full((8, 128), seventh * in_z[z], F32)
        weight_side[z] = in_y * (seventh * in_z[z])
    for level in range(STEPS):
        advance(level)
        keep_split(level + 1)
    store = pltpu.make_async_copy(xcat, kept, load_sem.at[0])
    store.start()

    wt = xcat[8 * HIST:8 * (HIST + COLS), 0:1024]
    wl = xcat[8 * HIST:8 * (HIST + COLS), 1024:2048]
    xt, xl = xcat[:, 0:1024], xcat[:, 1024:2048]
    pairs = bdot(xt, wt, NT) + bdot(xt, wl, NT) + bdot(xl, wt, NT) + bdot(xl, wl, NT)
    c_loc[0], c_loc[1] = fold_basis(pairs)
    csum.start_pair()
    hear(4, 5)
    gsum.start_line()
    csum.start_plane()
    leave(second)
    csum.start_line()
    gsum.start_share()
    store.wait()
    sums[2], sums[3] = gsum.result()
    gsum.finish()
    gsum.last().wait_send()
    csum.start_share()
    csum.finish()
    sums[0], sums[1] = csum.result()
    csum.last().wait_send()


def finish_kernel(cells, kept, sums, new_basis, r_out, xcat, done, r_factor, load_sem, store_sem):
    load = pltpu.make_async_copy(kept, xcat, load_sem.at[0])
    load.start()
    scale = 1.0 / cells
    one, two, three, four = [sums[k] * scale for k in range(4)]
    gram_h, right_h = unfold_history([three, four])
    lane = iota((24, 128), 1)
    row = iota((24, 128), 0)
    coef, own = unfold_basis(one, two)
    work = fdot(coef[:, 0:HIST], gram_h, NN) + fdot(coef, jnp.concatenate([right_h, jnp.zeros((72, 128), F32)], axis=0), NT)
    wide = jnp.concatenate([coef, jnp.zeros((104, 128), F32)], axis=0)
    gram = fdot(work - 2.0 * coef, wide, NT) + own
    rhs = jnp.where(lane < HIST, -coef, jnp.where(lane - HIST == row, 1.0, 0.0))

    columns = [jnp.broadcast_to(gram[:, k:k + 1], (24, 128)) for k in range(COLS)]
    lower = jnp.zeros((24, 128), F32)
    for j in range(COLS):
        pivot = jnp.broadcast_to(columns[j][j:j + 1], (24, 128))
        inverse = lax.rsqrt(pivot)
        inverse = inverse * (1.5 - 0.5 * pivot * inverse * inverse)
        column = jnp.where(row >= j, columns[j] * inverse, 0.0)
        lower = jnp.where(lane == j, column, lower)
        solved = jnp.broadcast_to(rhs[j:j + 1], (24, 128)) * inverse
        rhs = jnp.where(row == j, solved, rhs - jnp.where(row > j, column * solved, 0.0))
        for k in range(j + 1, COLS):
            columns[k] = columns[k] - column * jnp.broadcast_to(column[k:k + 1], (24, 128))
    square = jnp.concatenate([lower, jnp.zeros((104, 128), F32)], axis=0)
    r_factor[...] = square.T[0:COLS, 0:COLS]
    store_r = pltpu.make_async_copy(r_factor, r_out, store_sem.at[4])
    store_r.start()

    weights = rhs[0:COLS]
    top, low = split(weights)
    spread = ((iota((128, 8 * (HIST + COLS)), 1) // 8) == iota((128, 8 * (HIST + COLS)), 0)).astype(BF16)
    size = (8 * COLS, 8 * (HIST + COLS))
    same = (iota(size, 0) % 8) == (iota(size, 1) % 8)

    def widen(part):
        wide = bdot(part, spread, NN)
        wide = jnp.broadcast_to(wide[:, None, :], (COLS, 8, size[1])).reshape(size)
        return jnp.where(same, wide, 0.0).astype(BF16)

    top, low = widen(top), widen(low)
    load.wait()
    stores = []
    for part in range(4):
        cols = slice(256 * part, 256 * (part + 1))
        lows = slice(1024 + 256 * part, 1024 + 256 * (part + 1))
        out = bdot(top, xcat[:, cols], NN) + bdot(top, xcat[:, lows], NN) + bdot(low, xcat[:, cols], NN)
        for half in range(2):
            done[:, 2 * part + half] = out[:, 128 * half:128 * (half + 1)].reshape(COLS, 8, 128)
        layers = pl.ds(2 * part, 2)
        stores.append(pltpu.make_async_copy(done.at[:, layers], new_basis.at[:, layers], store_sem.at[part]))
        stores[-1].start()
    for copy in stores:
        copy.wait()
    store_r.wait()


def on_device(nx, ny, nz, history, start, diagonal):
    dma = pltpu.SemaphoreType.DMA
    tiles = lambda *shape: pltpu.VMEM((*shape, 8, 128), F32)
    plane = (nx // 2) * nz
    reduction = [tiles(2), tiles(), tiles(plane), tiles(ny), tiles(2)]
    any_spec = pl.BlockSpec(memory_space=pl.ANY)
    vmem = pl.BlockSpec(memory_space=pltpu.VMEM)
    cells = float(nx * ny * nz * diagonal.size)
    kept, sums = pl.pallas_call(
        functools.partial(cycle_kernel, nx, ny, nz),
        name="cycle",
        out_shape=(
            jax.ShapeDtypeStruct((8 * (HIST + COLS), 2048), BF16),
            jax.ShapeDtypeStruct((4, 8, 128), F32),
        ),
        in_specs=[any_spec] * 3,
        out_specs=(any_spec, vmem),
        scratch_shapes=[
            pltpu.VMEM((8 * (HIST + COLS), 2048), BF16),
            tiles(HIST, 8),
            tiles(1 + COLS, 16),
            tiles(1 + NRHS * STEPS, 16),
            tiles(1 + NRHS * STEPS),
            tiles(1 + NRHS * STEPS),
            tiles(1 + NRHS),
            tiles(2, 1 + NRHS),
            tiles(1 + NRHS),
            tiles(2, 1 + NRHS),
            tiles(3, 1 + NRHS),
            tiles(16),
            tiles(16),
            *reduction,
            *reduction,
            dma((3,)), pltpu.SemaphoreType.REGULAR((6,)), dma((18,)), dma((18,)),
            *[dma((2 + plane + ny,))] * 4,
        ],
        compiler_params=pltpu.CompilerParams(
            collective_id=0, has_side_effects=True, vmem_limit_bytes=VMEM_BYTES
        ),
    )(history, start, diagonal)
    return pl.pallas_call(
        functools.partial(finish_kernel, cells),
        name="finish",
        out_shape=(
            jax.ShapeDtypeStruct((COLS, 8, 8, 128), F32),
            jax.ShapeDtypeStruct((COLS, COLS), F32),
        ),
        in_specs=[any_spec, vmem],
        out_specs=(any_spec, any_spec),
        scratch_shapes=[
            pltpu.VMEM((8 * (HIST + COLS), 2048), BF16),
            tiles(COLS, 8),
            pltpu.VMEM((COLS, COLS), F32),
            dma((1,)),
            dma((5,)),
        ],
        compiler_params=pltpu.CompilerParams(vmem_limit_bytes=VMEM_BYTES),
    )(kept, sums)


def solution(mesh):
    return jax.shard_map(
        functools.partial(on_device, mesh.shape["gx"], mesh.shape["gy"], mesh.shape["gz"]),
        mesh=mesh,
        in_specs=(P(None, "gz", "gy", "gx"), P(None, "gz", "gy", "gx"), P("gz", "gy", "gx")),
        out_specs=(P(None, "gz", "gy", "gx"), P()),
        check_vma=False,
    )
```

```python
import functools

import jax
import jax.numpy as jnp
from jax import lax
from jax.experimental import pallas as pl
from jax.experimental.pallas import tpu as pltpu
from jax.sharding import PartitionSpec as P

STEPS = 4
NRHS = 4
HIST = 56
COLS = 20
MESH = pl.DeviceIdType.MESH
F32 = jnp.float32
BF16 = jnp.bfloat16
NT = (((1,), (1,)), ((), ()))
NN = (((1,), (0,)), ((), ()))
HIGH = lax.Precision.HIGHEST
VMEM_BYTES = 56_520_000


def iota(shape, dim):
    return lax.broadcasted_iota(jnp.int32, shape, dim)


def split(value):
    top = value.astype(BF16)
    return top, (value - top.astype(F32)).astype(BF16)


def bdot(left, right, dims):
    return lax.dot_general(left, right, dims, preferred_element_type=F32)


def fdot(left, right, dims):
    return lax.dot_general(left, right, dims, precision=HIGH, preferred_element_type=F32)


def both_products(left, right):
    swapped = jnp.concatenate([right[:, 1024:2048], right[:, 0:1024]], axis=1)
    return bdot(left, right, NT) + bdot(left, swapped, NT)


def keep_same_row(value):
    same = (iota(value.shape, 0) % 8) == (iota(value.shape, 1) % 8)
    masked = jnp.where(same, value, 0.0)
    return jnp.sum(masked.reshape(value.shape[0] // 8, 8, value.shape[1]), axis=1)


def thirds(value):
    first = value.astype(BF16)
    rest = value - first.astype(F32)
    second = rest.astype(BF16)
    return first, second, (rest - second.astype(F32)).astype(BF16)


class Total:
    def __init__(self, sizes, loc, inp, plane, line, out, send, recv):
        self.nx, self.ny, self.nz = sizes
        self.loc, self.inp, self.plane, self.line, self.out = loc, inp, plane, line, out
        self.send, self.recv = send, recv
        self.ix, self.iy, self.iz = lax.axis_index("gx"), lax.axis_index("gy"), lax.axis_index("gz")
        self.core = lax.rem(self.ix, 2)
        self.iyc = self.ix // 2

    def pair_copy(self, src, dst, number):
        return pltpu.make_async_remote_copy(
            src_ref=src, dst_ref=dst, send_sem=self.send.at[number], recv_sem=self.recv.at[number],
            device_id={"gx": self.ix + 1 - 2 * self.core}, device_id_type=MESH,
        )

    def plane_copies(self):
        nyc, nz = self.nx // 2, self.nz
        for step in range(1, nyc * nz):
            py = lax.rem(self.iyc + step // nz, nyc)
            pz = lax.rem(self.iz + step % nz, nz)
            yield py * nz + pz, self.iyc * nz + self.iz, {"gx": 2 * py + self.core, "gz": pz}, 2 + step

    def line_copies(self):
        for step in range(1, self.ny):
            peer = lax.rem(self.iy + step, self.ny)
            yield peer, self.iy, {"gy": peer}, 2 + (self.nx // 2) * self.nz + step

    def spread(self, copies, buf, base):
        for peer, me, device, number in copies:
            pltpu.make_async_remote_copy(
                src_ref=buf.at[me], dst_ref=buf.at[me], send_sem=self.send.at[number],
                recv_sem=self.recv.at[base + me], device_id=device, device_id_type=MESH,
            ).start()

    def collect(self, copies, buf, base):
        for peer, _, device, number in copies:
            pltpu.make_async_remote_copy(
                src_ref=buf.at[peer], dst_ref=buf.at[peer], send_sem=self.send.at[number],
                recv_sem=self.recv.at[base + peer], device_id=device, device_id_type=MESH,
            ).wait_recv()

    def drain(self, copies, buf, base):
        for peer, me, device, number in copies:
            pltpu.make_async_remote_copy(
                src_ref=buf.at[me], dst_ref=buf.at[me], send_sem=self.send.at[number],
                recv_sem=self.recv.at[base + me], device_id=device, device_id_type=MESH,
            ).wait_send()

    def first(self):
        return self.pair_copy(self.loc.at[1 - self.core], self.inp, 0)

    def last(self):
        return self.pair_copy(self.out.at[self.core], self.out.at[self.core], 1)

    def start_pair(self):
        self.first().start()

    def start_plane(self):
        self.first().wait_recv()
        self.plane[self.iyc * self.nz + self.iz] = self.loc[self.core] + self.inp[...]
        self.spread(self.plane_copies(), self.plane, 2)

    def start_line(self):
        self.collect(self.plane_copies(), self.plane, 2)
        self.line[self.iy] = total_of(self.plane)
        self.spread(self.line_copies(), self.line, 2 + (self.nx // 2) * self.nz)

    def start_share(self):
        self.collect(self.line_copies(), self.line, 2 + (self.nx // 2) * self.nz)
        self.out[self.core] = total_of(self.line)
        self.last().start()

    def result(self):
        other = self.out.at[1 - self.core]
        self.pair_copy(other, other, 1).wait_recv()
        return self.out[0], self.out[1]

    def finish(self):
        self.first().wait_send()
        self.drain(self.plane_copies(), self.plane, 2)
        self.drain(self.line_copies(), self.line, 2 + (self.nx // 2) * self.nz)


def total_of(ref):
    parts = [ref[place] for place in range(ref.shape[0])]
    while len(parts) > 1:
        parts = [sum(parts[k:k + 2][1:], parts[k]) for k in range(0, len(parts), 2)]
    return parts[0]


def fold_history(pairs):
    rows = jnp.concatenate(thirds(keep_same_row(pairs)), axis=0)
    pick = ((iota((8 * HIST, 128), 0) // 8) == iota((8 * HIST, 128), 1)).astype(BF16)
    parts = bdot(rows, pick, NN)
    full = parts[0:HIST] + parts[HIST:2 * HIST] + parts[2 * HIST:3 * HIST]
    lane = iota((8, 128), 1)
    tiles = []
    for half in range(2):
        low = 8 * half
        tile = jnp.where(lane < 56, full[low:low + 8], 0.0)
        tile = jnp.where((lane >= 56) & (lane < 96), pltpu.roll(full[16 + low:24 + low], 40, 1), tile)
        tile = jnp.where((lane >= 96) & (lane < 120), pltpu.roll(full[32 + low:40 + low], 64, 1), tile)
        if half == 0:
            tile = jnp.where(lane >= 120, pltpu.roll(full[48:56], 72, 1), tile)
        tiles.append(tile)
    return tiles


def unfold_history(tiles):
    lane = iota((8, 128), 1)
    rows = []
    for first, turn in ((0, 0), (16, 88), (32, 64), (48, 56)):
        for tile in tiles[:1] if first == 48 else tiles:
            turned = tile if turn == 0 else pltpu.roll(tile, turn, 1)
            rows.append(jnp.where((lane >= first) & (lane < HIST), turned, 0.0))
    upper = jnp.concatenate(rows, axis=0)
    right = jnp.where(iota((HIST, 128), 1) >= 16 * (iota((HIST, 128), 0) // 16) + 16, upper, 0.0)
    return upper, right


def fold_basis(pairs):
    rows = keep_same_row(pairs)
    rows = jnp.concatenate([rows, jnp.zeros((128 - HIST - COLS, 8 * COLS), F32)], axis=0)
    rows = jnp.concatenate(thirds(rows), axis=0)
    pick = (iota((24, 8 * COLS), 0) == (iota((24, 8 * COLS), 1) // 8)).astype(BF16)
    parts = bdot(pick, rows, NT)
    full = parts[:, 0:128] + parts[:, 128:256] + parts[:, 256:384]
    lane = iota((8, 128), 1)
    one = jnp.where(lane < HIST, full[0:8], jnp.where(lane >= 64, pltpu.roll(full[8:16], 64, 1), 0.0))
    two = jnp.where(lane < HIST, full[16:24], 0.0)
    for part in range(3):
        first = 64 + 20 * part
        turned = pltpu.roll(full[8 * part:8 * part + 8], first - HIST, 1)
        two = jnp.where((lane >= first) & (lane < first + COLS), turned, two)
    return one, two


def unfold_basis(one, two):
    lane = iota((24, 128), 1)
    coef = jnp.concatenate([one, pltpu.roll(one, 64, 1), two], axis=0)
    own = jnp.concatenate([pltpu.roll(two, 128 - 64 - 20 * part, 1) for part in range(3)], axis=0)
    return jnp.where(lane < HIST, coef, 0.0), jnp.where(lane < COLS, own, 0.0)


def cycle_kernel(
    nx, ny, nz,
    hist_hbm, start_hbm, diag_hbm,
    kept, sums,
    xcat, hbuf, main, side, edge, corner, x_send, x_recv, x_own, e_recv, k_recv, weight_main, weight_side,
    g_loc, g_inp, g_plane, g_line, g_out,
    c_loc, c_inp, c_plane, c_line, c_out,
    load_sem, heard, hs_sem, hr_sem, g_send, g_recv, c_send, c_recv,
):
    sizes = (nx, ny, nz)
    gsum = Total(sizes, g_loc, g_inp, g_plane, g_line, g_out, g_send, g_recv)
    csum = Total(sizes, c_loc, c_inp, c_plane, c_line, c_out, c_send, c_recv)
    ix, iy, iz = lax.axis_index("gx"), lax.axis_index("gy"), lax.axis_index("gz")
    load_w = pltpu.make_async_copy(start_hbm, main.at[pl.ds(1, NRHS), pl.ds(4, 8)], load_sem.at[0])
    load_d = pltpu.make_async_copy(diag_hbm, main.at[0, pl.ds(4, 8)], load_sem.at[1])
    load_h = pltpu.make_async_copy(hist_hbm, hbuf, load_sem.at[2])
    load_w.start()
    load_d.start()
    load_h.start()

    barrier = pltpu.get_barrier_semaphore()
    nyc, core = nx // 2, lax.rem(ix, 2)
    reach = max(1, ny // 8)

    def far_off(dy, dz):
        return {"gx": 2 * lax.rem(ix // 2 + dy, nyc) + core, "gz": lax.rem(iz + dz, nz)}

    def hops(step, count):
        return min(step, count - step)

    greeted = [{"gx": lax.rem(ix + 1, nx)}, {"gx": lax.rem(ix + nx - 1, nx)}]
    for dy in range(nyc):
        for dz in range(nz):
            if 1 <= hops(dy, nyc) + hops(dz, nz) <= 2:
                greeted.append(far_off(dy, dz))
    for step in range(1, reach + 1):
        greeted += [{"gy": lax.rem(iy + step, ny)}, {"gy": lax.rem(iy + ny - step, ny)}]
    for dy in (1, ny - 1):
        for dz in (1, nz - 1):
            greeted.append({"gy": lax.rem(iy + dy, ny), "gz": lax.rem(iz + dz, nz)})

    def tell(number, device):
        pl.semaphore_signal(heard.at[number], inc=1, device_id=device, device_id_type=MESH)

    def tell_line(number, step):
        tell(number, {"gy": lax.rem(iy + step, ny)})
        tell(number + 1, {"gy": lax.rem(iy + ny - step, ny)})

    def hear(*numbers):
        for number in numbers:
            pl.semaphore_wait(heard.at[number], 1)

    low_x, high_x = ix == 0, ix == nx - 1
    low_y, high_y = iy == 0, iy == ny - 1
    low_z, high_z = iz == 0, iz == nz - 1
    places = 1 + NRHS
    zero = jnp.zeros((places, 8, 128), F32)
    half = jnp.zeros((places, 4, 128), F32)
    side[0:places, 0] = zero
    side[0:places, 15] = zero
    for at, outside in ((0, low_x), (1, high_x)):
        @pl.when(outside)
        def _():
            x_recv[at] = zero
    for at, outside in ((0, low_y), (1, high_y)):
        rows = pl.ds(4 - 4 * at, 4)

        @pl.when(outside)
        def _():
            for z in range(1, 15):
                side[0:places, z, rows] = half
            for third in range(3):
                k_recv[third, :, rows] = half
    for at, outside in ((0, low_z), (1, high_z)):
        @pl.when(outside)
        def _():
            e_recv[at] = zero
            k_recv[1 + at] = zero
            for z in range(12 * at, 12 * at + 4):
                main[0:places, z] = zero
                side[0:places, z] = zero

    for device in greeted:
        pl.semaphore_signal(barrier, inc=1, device_id=device, device_id_type=MESH)

    lane = iota((8, 128), 1)
    row = iota((8, 128), 0)

    def there(dx, dy, dz):
        out = jnp.bool_(True)
        for step, me, count in ((dx, ix, nx), (dy, iy, ny), (dz, iz, nz)):
            if step:
                out = jnp.logical_and(out, me + step >= 0 if step < 0 else me + step < count)
        return out

    def message(number, dx, dy, dz, src, dst):
        device = {}
        for axis, step, me, count in (("gx", dx, ix, nx), ("gy", dy, iy, ny), ("gz", dz, iz, nz)):
            if step:
                device[axis] = lax.rem(me + step + count, count)
        copy = pltpu.make_async_remote_copy(
            src_ref=src, dst_ref=dst, send_sem=hs_sem.at[number], recv_sem=hr_sem.at[number],
            device_id=device, device_id_type=MESH,
        )
        return there(dx, dy, dz), there(-dx, -dy, -dz), copy

    few = pl.ds(0, places)
    rows_of = {1: pl.ds(4, 4), -1: pl.ds(0, 4)}
    first = [message(0, 1, 0, 0, x_send, x_recv.at[0]), message(1, -1, 0, 0, x_send, x_recv.at[1])]
    first.append(message(2, 0, 0, 1, main.at[few, pl.ds(8, 4)], main.at[few, pl.ds(0, 4)]))
    first.append(message(3, 0, 0, -1, main.at[few, pl.ds(4, 4)], main.at[few, pl.ds(12, 4)]))
    second = [message(4, 0, 0, 1, x_own, e_recv.at[0]), message(5, 0, 0, -1, x_own, e_recv.at[1])]
    for k, dy in enumerate((1, -1)):
        rows = rows_of[dy]
        first.append(message(
            6 + k, 0, dy, 0, main.at[few, pl.ds(4, 8), rows], side.at[few, pl.ds(4, 8), rows]))
        second.append(message(8 + k, 0, dy, 0, x_own.at[:, rows], k_recv.at[0, :, rows]))
        for n, dz in enumerate((1, -1)):
            src = pl.ds(9 if dz > 0 else 4, 3)
            dst = pl.ds(1 if dz > 0 else 12, 3)
            first.append(message(
                10 + 2 * k + n, 0, dy, dz, main.at[few, src, rows], side.at[few, dst, rows]))
            second.append(message(14 + 2 * k + n, 0, dy, dz, x_own.at[:, rows], k_recv.at[1 + n, :, rows]))

    def send(messages):
        for sends, _, copy in messages:
            @pl.when(sends)
            def _():
                copy.start()

    def receive(messages):
        for _, comes, copy in messages:
            @pl.when(comes)
            def _():
                copy.wait_recv()

    def leave(messages):
        for sends, _, copy in messages:
            @pl.when(sends)
            def _():
                copy.wait_send()

    def keep_split(level):
        for z in range(8):
            block = main[1 + NRHS * level:1 + NRHS * (level + 1), 4 + z].reshape(8 * NRHS, 128)
            top, low = split(block)
            rows = pl.ds(8 * (HIST + NRHS * level), 8 * NRHS)
            xcat[rows, 128 * z:128 * (z + 1)] = top
            xcat[rows, 1024 + 128 * z:1024 + 128 * (z + 1)] = low

    def turn(value, by, axis):
        by = by % value.shape[axis]
        return value if by == 0 else pltpu.roll(value, by, axis)

    inside = lambda outside: jnp.where(outside, 0.0, 1.0).astype(F32)
    in_z = [inside(low_z) if z < 4 else (inside(high_z) if z > 11 else 1.0) for z in range(16)]
    in_y = jnp.where(row < 4, inside(high_y), inside(low_y))
    in_x = jnp.where(lane % 8 < 4, inside(high_x), inside(low_x))
    in_x = in_x * jnp.where((lane >= 28) & (lane < 92), 1.0, jnp.where((lane >= 92) & (lane < 124), in_z[12], in_z[0]))
    seventh = 1.0 / 7.0

    def beside_x(value, turned):
        at = iota(value.shape, 2)
        left = turn(jnp.where(at == 127, turned, value), 1, 2)
        return left + turn(jnp.where(at == 0, turned, value), -1, 2)

    def beside_y(inner, outer):
        at = iota(inner.shape, inner.ndim - 2)
        inner_low, outer_low = turn(inner, 1, inner.ndim - 2), turn(outer, 1, inner.ndim - 2)
        inner_high, outer_high = turn(inner, -1, inner.ndim - 2), turn(outer, -1, inner.ndim - 2)
        return (
            jnp.where(at == 0, outer_low, inner_low) + jnp.where(at == 7, outer_high, inner_high),
            jnp.where(at == 0, inner_low, outer_low) + jnp.where(at == 7, inner_high, outer_high),
        )

    def beside_edge(value, ends):
        left = jnp.where(lane % 8 == 0, turn(ends, 1, 1), turn(value, 1, 1))
        right = jnp.where(lane % 8 == 7, turn(ends, -1, 1), turn(value, -1, 1))
        return left + right + turn(value, 8, 1) + turn(value, -8, 1)

    def spread(value, low, high):
        return jnp.concatenate([turn(value, -8 * z, 1)[None] for z in range(low, high)], axis=0)

    def ends_of(base, value, low, high):
        turned = [turn(value[z - low], 8 * z, 1) for z in range(low, high)]
        for z in range(low, high):
            base = jnp.where((lane == 8 * z) | (lane == (8 * z + 127) % 128), turned[z - low], base)
        return base

    def advance(level):
        more = level < STEPS - 1
        low, high = level + 1, 15 - level

        def vector(f, carry):
            at = 1 + NRHS * level + f

            def follow(scaled, ref, *place):
                if level > 0:
                    scaled = 2.0 * scaled - ref[(at - NRHS, *place)]
                ref[(at + NRHS, *place)] = scaled

            v, u = main[at, low:high], side[at, low:high]
            edge_v, corner_v = edge[at], corner[at]
            turned = spread(edge_v, low, high)
            if more:
                turned_u = spread(corner_v, low + 1, high - 1)
                ends = ends_of(edge_v, v, low, high)
                side_ends = ends_of(corner_v, u, low, high)
            across = beside_x(v, turned)
            if more:
                across_u = beside_x(u[1:-1], turned_u)
            near, far = beside_y(v, u)
            near = near + across + main[at, low - 1:high - 1] + main[at, low + 1:high + 1]
            follow(main[0, low:high] * v - near * weight_main[low:high], main, slice(low, high))
            if more:
                far = far[1:-1] + across_u + side[at, low:high - 2] + side[at, low + 2:high]
                follow(
                    side[0, low + 1:high - 1] * u[1:-1] - far * weight_side[low + 1:high - 1],
                    side, slice(low + 1, high - 1),
                )
                near, far = beside_y(edge_v, corner_v)
                near = near + beside_edge(edge_v, ends)
                far = far + beside_edge(corner_v, side_ends)
                follow(edge[0] * edge_v - near * (in_x * seventh), edge)
                follow(corner[0] * corner_v - far * (in_x * in_y * seventh), corner)
            return carry

        lax.fori_loop(0, NRHS, vector, 0, unroll=4)

    load_w.wait()
    load_d.wait()
    for place in range(places):
        packed = jnp.zeros((8, 128), F32)
        for z in range(4, 12):
            here = (lane >= 8 * z - 4) & (lane < 8 * z + 4)
            packed = jnp.where(here, turn(main[place, z], 8 * z, 1), packed)
        x_send[place] = packed
    pl.semaphore_wait(barrier, len(greeted))
    send(first)
    if nyc > 1:
        tell(0, far_off(nyc // 2, 0))
    if nz > 1:
        tell(1, far_off(0, nz // 2))
    tell_line(2, reach)

    load_h.wait()
    for z in range(8):
        top, low = split(hbuf[:, z].reshape(8 * HIST, 128))
        xcat[0:8 * HIST, 128 * z:128 * (z + 1)] = top
        xcat[0:8 * HIST, 1024 + 128 * z:1024 + 128 * (z + 1)] = low
    receive(first[:2])
    for place in range(places):
        x_own[place] = jnp.where(lane % 8 >= 4, x_recv[0, place], x_recv[1, place])
    send(second)
    hear(2, 3)
    tell_line(4, 2 * reach)
    pairs = both_products(xcat[0:8 * HIST], xcat[0:8 * HIST])
    g_loc[0], g_loc[1] = fold_history(pairs)
    gsum.start_pair()
    keep_split(0)

    receive(first[2:])
    receive(second)
    leave(first)
    hear(*([0] if nyc > 1 else []), *([1] if nz > 1 else []))
    gsum.start_plane()
    own = (lane >= 28) & (lane < 92)
    for place in range(places):
        above = turn(jnp.where(lane < 60, e_recv[1, place], e_recv[0, place]), 64, 1)
        edge[place] = jnp.where(own, x_own[place], above)
        above = turn(jnp.where(lane < 60, k_recv[2, place], k_recv[1, place]), 64, 1)
        corner[place] = jnp.where(own, k_recv[0, place], above)
    for z in range(1, 15):
        scaled = (main[0, z] - 1.0) * seventh
        main[0, z] = scaled if 4 <= z < 12 else scaled * in_z[z]
        scaled = (side[0, z] - 1.0) * (in_y * seventh)
        side[0, z] = scaled if 4 <= z < 12 else scaled * in_z[z]
    edge[0] = (edge[0] - 1.0) * (in_x * seventh)
    corner[0] = (corner[0] - 1.0) * (in_x * in_y * seventh)
    for z in range(16):
        weight_main[z] = jnp.full((8, 128), seventh * in_z[z], F32)
        weight_side[z] = in_y * (seventh * in_z[z])
    for level in range(STEPS):
        advance(level)
        keep_split(level + 1)
    store = pltpu.make_async_copy(xcat, kept, load_sem.at[0])
    store.start()

    pairs = both_products(xcat[...], xcat[8 * HIST:8 * (HIST + COLS)])
    c_loc[0], c_loc[1] = fold_basis(pairs)
    csum.start_pair()
    hear(4, 5)
    gsum.start_line()
    csum.start_plane()
    leave(second)
    csum.start_line()
    gsum.start_share()
    store.wait()
    sums[2], sums[3] = gsum.result()
    gsum.finish()
    gsum.last().wait_send()
    csum.start_share()
    csum.finish()
    sums[0], sums[1] = csum.result()
    csum.last().wait_send()


def finish_kernel(cells, kept, sums, new_basis, r_out, xcat, done, r_factor, load_sem, store_sem):
    load = pltpu.make_async_copy(kept, xcat, load_sem.at[0])
    load.start()
    scale = 1.0 / cells
    one, two, three, four = [sums[k] * scale for k in range(4)]
    gram_h, right_h = unfold_history([three, four])
    lane = iota((24, 128), 1)
    row = iota((24, 128), 0)
    coef, own = unfold_basis(one, two)
    work = fdot(coef[:, 0:HIST], gram_h, NN) + fdot(coef, jnp.concatenate([right_h, jnp.zeros((72, 128), F32)], axis=0), NT)
    wide = jnp.concatenate([coef, jnp.zeros((104, 128), F32)], axis=0)
    gram = fdot(work - 2.0 * coef, wide, NT) + own
    rhs = jnp.where(lane < HIST, -coef, jnp.where(lane - HIST == row, 1.0, 0.0))

    columns = [jnp.broadcast_to(gram[:, k:k + 1], (24, 128)) for k in range(COLS)]
    lower = jnp.zeros((24, 128), F32)
    for j in range(COLS):
        pivot = jnp.broadcast_to(columns[j][j:j + 1], (24, 128))
        inverse = lax.rsqrt(pivot)
        inverse = inverse * (1.5 - 0.5 * pivot * inverse * inverse)
        column = jnp.where(row >= j, columns[j] * inverse, 0.0)
        lower = jnp.where(lane == j, column, lower)
        solved = jnp.broadcast_to(rhs[j:j + 1], (24, 128)) * inverse
        rhs = jnp.where(row == j, solved, rhs - jnp.where(row > j, column * solved, 0.0))
        for k in range(j + 1, COLS):
            columns[k] = columns[k] - column * jnp.broadcast_to(column[k:k + 1], (24, 128))
    square = jnp.concatenate([lower, jnp.zeros((104, 128), F32)], axis=0)
    r_factor[...] = square.T[0:COLS, 0:COLS]
    store_r = pltpu.make_async_copy(r_factor, r_out, store_sem.at[4])
    store_r.start()

    weights = rhs[0:COLS]
    top, low = split(weights)
    spread = ((iota((128, 8 * (HIST + COLS)), 1) // 8) == iota((128, 8 * (HIST + COLS)), 0)).astype(BF16)
    size = (8 * COLS, 8 * (HIST + COLS))
    same = (iota(size, 0) % 8) == (iota(size, 1) % 8)

    def widen(part):
        wide = bdot(part, spread, NN)
        wide = jnp.broadcast_to(wide[:, None, :], (COLS, 8, size[1])).reshape(size)
        return jnp.where(same, wide, 0.0).astype(BF16)

    top, low = widen(top), widen(low)
    load.wait()
    stores = []
    for part in range(4):
        cols = slice(256 * part, 256 * (part + 1))
        lows = slice(1024 + 256 * part, 1024 + 256 * (part + 1))
        out = bdot(top, xcat[:, cols], NN) + bdot(top, xcat[:, lows], NN) + bdot(low, xcat[:, cols], NN)
        for half in range(2):
            done[:, 2 * part + half] = out[:, 128 * half:128 * (half + 1)].reshape(COLS, 8, 128)
        layers = pl.ds(2 * part, 2)
        stores.append(pltpu.make_async_copy(done.at[:, layers], new_basis.at[:, layers], store_sem.at[part]))
        stores[-1].start()
    for copy in stores:
        copy.wait()
    store_r.wait()


def on_device(nx, ny, nz, history, start, diagonal):
    dma = pltpu.SemaphoreType.DMA
    tiles = lambda *shape: pltpu.VMEM((*shape, 8, 128), F32)
    plane = (nx // 2) * nz
    reduction = [tiles(2), tiles(), tiles(plane), tiles(ny), tiles(2)]
    any_spec = pl.BlockSpec(memory_space=pl.ANY)
    vmem = pl.BlockSpec(memory_space=pltpu.VMEM)
    cells = float(nx * ny * nz * diagonal.size)
    kept, sums = pl.pallas_call(
        functools.partial(cycle_kernel, nx, ny, nz),
        name="cycle",
        out_shape=(
            jax.ShapeDtypeStruct((8 * (HIST + COLS), 2048), BF16),
            jax.ShapeDtypeStruct((4, 8, 128), F32),
        ),
        in_specs=[any_spec] * 3,
        out_specs=(any_spec, vmem),
        scratch_shapes=[
            pltpu.VMEM((8 * (HIST + COLS), 2048), BF16),
            tiles(HIST, 8),
            tiles(1 + COLS, 16),
            tiles(1 + NRHS * STEPS, 16),
            tiles(1 + NRHS * STEPS),
            tiles(1 + NRHS * STEPS),
            tiles(1 + NRHS),
            tiles(2, 1 + NRHS),
            tiles(1 + NRHS),
            tiles(2, 1 + NRHS),
            tiles(3, 1 + NRHS),
            tiles(16),
            tiles(16),
            *reduction,
            *reduction,
            dma((3,)), pltpu.SemaphoreType.REGULAR((6,)), dma((18,)), dma((18,)),
            *[dma((2 + plane + ny,))] * 4,
        ],
        compiler_params=pltpu.CompilerParams(
            collective_id=0, has_side_effects=True, vmem_limit_bytes=VMEM_BYTES
        ),
    )(history, start, diagonal)
    return pl.pallas_call(
        functools.partial(finish_kernel, cells),
        name="finish",
        out_shape=(
            jax.ShapeDtypeStruct((COLS, 8, 8, 128), F32),
            jax.ShapeDtypeStruct((COLS, COLS), F32),
        ),
        in_specs=[any_spec, vmem],
        out_specs=(any_spec, any_spec),
        scratch_shapes=[
            pltpu.VMEM((8 * (HIST + COLS), 2048), BF16),
            tiles(COLS, 8),
            pltpu.VMEM((COLS, COLS), F32),
            dma((1,)),
            dma((5,)),
        ],
        compiler_params=pltpu.CompilerParams(vmem_limit_bytes=VMEM_BYTES),
    )(kept, sums)


def solution(mesh):
    return jax.shard_map(
        functools.partial(on_device, mesh.shape["gx"], mesh.shape["gy"], mesh.shape["gz"]),
        mesh=mesh,
        in_specs=(P(None, "gz", "gy", "gx"), P(None, "gz", "gy", "gx"), P("gz", "gy", "gx")),
        out_specs=(P(None, "gz", "gy", "gx"), P()),
        check_vma=False,
    )
```
